512 devices in a mesh: seq: 32 (over x, y, core), tensor: 16 (over z).
Axes of the slice: x: 4, y: 4, z: 16, core: 2. Of those that a mesh axis runs over, the one named last changes fastest.
Arguments:
- byte_states: bfloat16 [32768, 1024], P('seq'), may hold values from -6 to 6
- byte_patch: int32 [32768], P('seq'), may hold values from 0 to 4095, as said below
- patch_len: int32 [4096], replicated, may hold values from 1 to 1024, as said below
- cross_query: bfloat16 [1024, 4096], P('seq', 'tensor'), may hold values from -0.75 to 0.75
- cross_key: bfloat16 [1024, 4096], P('seq', 'tensor'), may hold values from -0.375 to 0.375
- cross_value: bfloat16 [1024, 4096], P('seq', 'tensor'), may hold values from -0.1875 to 0.1875
- cross_out: bfloat16 [4096, 4096], P('tensor', 'seq'), may hold values from -0.09375 to 0.09375
- norm_gain: float32 [4096], replicated, may hold values from 0.5 to 1.5
- latent_query: bfloat16 [4096, 4096], P('seq', 'tensor'), may hold values from -0.1875 to 0.1875
- latent_key: bfloat16 [4096, 4096], P('seq', 'tensor'), may hold values from -0.1875 to 0.1875
- latent_value: bfloat16 [4096, 4096], P('seq', 'tensor'), may hold values from -0.09375 to 0.09375
- latent_out: bfloat16 [4096, 4096], P('tensor', 'seq'), may hold values from -0.09375 to 0.09375
Outputs:
- patch_latent: bfloat16 [4096, 4096], P('seq', 'tensor')
The draws below stay inside these ranges and needn't reach their ends.
Inputs may be any that keep to these rules, and one draw needn't show every extreme that they name: `byte_patch`: within each aligned block of 1024 bytes the numbers never fall and rise by at most one from byte to byte, and the block's first byte starts a new patch, so no patch spans two blocks. Block k begins with patch number k * 128 + r with -64 <= r < 64; the first block begins with 0 and the last ends with 4095. A block holds 1 to 255 patches; some block holds exactly 255 and the block after it exactly one. patch_len[p] is the number of bytes b with byte_patch[b] = p.
All inputs are finite; a program needn't handle non-finite values.
Results may differ from the reference program's by a relative error of at most 0.028.
Values may be sent and summed in bfloat16 or wider, within the bound.
A program may use at most 64 MiB of HBM per device.

```python
import math
import jax
import jax.numpy as jnp
from jax import lax

DB = 1024
D = 4096
HEADS = 32
HEAD_DIM = 128
PATCH_DEV = 128
BYTE_DEV = 1024
BYTES = 32768
PATCHES = 4096


def patch_layout(key):
    folded = jax.random.fold_in(key, 7)
    shards = BYTES // BYTE_DEV
    half_width = PATCH_DEV // 2
    drift_key, pick_key, cut_key = jax.random.split(folded, 3)
    interior = jax.random.randint(drift_key, (shards + 1,), -half_width, half_width)
    forced = 1 + jax.random.randint(pick_key, (), 0, shards - 3)
    places = jnp.arange(shards + 1)
    drifts = jnp.where(places == forced, -half_width, interior)
    drifts = jnp.where(places == forced + 1, half_width - 1, drifts)
    drifts = jnp.where(places == forced + 2, -half_width, drifts)
    drifts = jnp.where((places == 0) | (places == shards), 0, drifts)
    counts = PATCH_DEV + drifts[1:] - drifts[:-1]
    firsts = jnp.arange(shards) * PATCH_DEV + drifts[:-1]
    shard_keys = jax.random.split(cut_key, shards)
    orders = jax.vmap(lambda single: jax.random.permutation(single, BYTE_DEV - 1))(shard_keys)
    cut_mask = orders < (counts - 1)[:, None]
    starts = jnp.concatenate([jnp.ones((shards, 1), jnp.int32), cut_mask.astype(jnp.int32)], axis=1)
    local_rank = jnp.cumsum(starts, axis=1) - 1
    return (firsts[:, None] + local_rank).reshape(BYTES).astype(jnp.int32)


def draw_byte_patch(key, part):
    return patch_layout(key)


def draw_patch_len(key, part):
    patches = patch_layout(key)
    return jax.ops.segment_sum(jnp.ones((BYTES,), jnp.int32), patches, num_segments=PATCHES).astype(jnp.int32)


def block_levels(stream_key, dims, pieces, smallest, largest):
    def one(dim, blocks):
        heights = jax.random.uniform(jax.random.fold_in(jax.random.fold_in(stream_key, 6), dim), (blocks,), jnp.float32, smallest / len(pieces), largest / len(pieces))
        return jnp.repeat(jnp.exp(heights), dims[dim] // blocks).reshape((-1,) + (1,) * (len(dims) - dim - 1))

    level = one(*pieces[0])
    for cut in pieces[1:]:
        level = level * one(*cut)
    return level


def noise(key, shape, spread, bound, pieces=(), held_as=jnp.bfloat16):
    factor_of = block_levels(key, shape, pieces, -0.22, 0.18) if pieces else 1.0
    result = jax.random.normal(key, shape, jnp.float32) * spread * factor_of
    return jnp.minimum(jnp.maximum(result, -bound), bound).astype(held_as)


def setup_inputs(seed: int = 0) -> dict:
    keys = jax.random.split(jax.random.key(seed), 13)
    return {
        "byte_states": noise(keys[0], (BYTES, DB), 1.0, 6.0, ((0, 32),)),
        "byte_patch": draw_byte_patch(jax.random.fold_in(keys[12], 71), 0),
        "patch_len": draw_patch_len(jax.random.fold_in(keys[12], 71), 0),
        "cross_query": noise(keys[3], (DB, HEADS * HEAD_DIM), (DB // 16) ** -0.5, 0.75, ((0, 32), (1, 16))),
        "cross_key": noise(keys[4], (DB, HEADS * HEAD_DIM), (DB // 4) ** -0.5, 0.375, ((0, 32), (1, 16))),
        "cross_value": noise(keys[5], (DB, HEADS * HEAD_DIM), DB ** -0.5, 0.1875, ((0, 32), (1, 16))),
        "cross_out": noise(keys[6], (HEADS * HEAD_DIM, D), (HEADS * HEAD_DIM) ** -0.5, 0.09375, ((0, 16), (1, 32))),
        "norm_gain": jnp.clip(1.0 + 0.1 * jax.random.normal(keys[7], (D,), jnp.float32), 0.5, 1.5),
        "latent_query": noise(keys[8], (D, HEADS * HEAD_DIM), (D // 4) ** -0.5, 0.1875, ((0, 32), (1, 16))),
        "latent_key": noise(keys[9], (D, HEADS * HEAD_DIM), (D // 4) ** -0.5, 0.1875, ((0, 32), (1, 16))),
        "latent_value": noise(keys[10], (D, HEADS * HEAD_DIM), D ** -0.5, 0.09375, ((0, 32), (1, 16))),
        "latent_out": noise(keys[11], (HEADS * HEAD_DIM, D), (HEADS * HEAD_DIM) ** -0.5, 0.09375, ((0, 16), (1, 32))),
    }


score_cap = 30.0
norm_eps = 1e-05

def capped_exp(scores):
    return jnp.exp(score_cap * jnp.tanh(scores / score_cap))

def rounded(value):
    return lax.optimization_barrier(value.astype(jnp.bfloat16))

def reference(byte_states, byte_patch, patch_len, cross_query, cross_key, cross_value, cross_out, norm_gain, latent_query, latent_key, latent_value, latent_out):
    inner_width = HEADS * HEAD_DIM
    byte_sums = jax.ops.segment_sum(byte_states.astype(jnp.float32), byte_patch, num_segments=PATCHES)
    pooled = rounded(byte_sums / patch_len.astype(jnp.float32)[:, None])
    cross_q = rounded(jnp.dot(pooled, cross_query, preferred_element_type=jnp.float32))
    cross_k = rounded(jnp.dot(byte_states, cross_key, preferred_element_type=jnp.float32))
    cross_v = rounded(jnp.dot(byte_states, cross_value, preferred_element_type=jnp.float32))
    query_bytes = jnp.take(cross_q, byte_patch, axis=0).astype(jnp.float32)
    scores = (query_bytes * cross_k.astype(jnp.float32)).reshape(BYTES, HEADS, HEAD_DIM).sum(axis=2) / math.sqrt(HEAD_DIM)
    byte_raw = capped_exp(scores)
    byte_total = jax.ops.segment_sum(byte_raw, byte_patch, num_segments=PATCHES)
    byte_weight = rounded(byte_raw / jnp.take(byte_total, byte_patch, axis=0))
    weighted = byte_weight.astype(jnp.float32)[:, :, None] * cross_v.astype(jnp.float32).reshape(BYTES, HEADS, HEAD_DIM)
    cross_heads = rounded(jax.ops.segment_sum(weighted.reshape(BYTES, inner_width), byte_patch, num_segments=PATCHES))
    latent_in = rounded(jnp.dot(cross_heads, cross_out, preferred_element_type=jnp.float32))
    hidden = latent_in.astype(jnp.float32)
    mean_square = lax.optimization_barrier(jnp.mean(hidden * hidden, axis=1, keepdims=True))
    normed = rounded(hidden * lax.rsqrt(mean_square + norm_eps) * norm_gain[None, :])
    latent_q = rounded(jnp.dot(normed, latent_query, preferred_element_type=jnp.float32))
    latent_k = rounded(jnp.dot(normed, latent_key, preferred_element_type=jnp.float32))
    latent_v = rounded(jnp.dot(normed, latent_value, preferred_element_type=jnp.float32))

    def split_heads(matrix):
        return matrix.reshape(PATCHES, HEADS, HEAD_DIM).transpose(1, 0, 2)
    positions = jnp.arange(PATCHES, dtype=jnp.int32)
    allowed = positions[None, :] <= positions[:, None]

    def head_attention(operands):
        head_q, head_k, head_v = operands
        head_scores = jnp.dot(head_q.astype(jnp.float32), head_k.astype(jnp.float32).T, preferred_element_type=jnp.float32) / math.sqrt(HEAD_DIM)
        attn_raw = jnp.where(allowed, capped_exp(head_scores), jnp.zeros_like(head_scores))
        attn_total = lax.optimization_barrier(jnp.sum(attn_raw, axis=1, keepdims=True))
        attn_weight = rounded(attn_raw)
        summed = jnp.dot(attn_weight.astype(jnp.float32), head_v.astype(jnp.float32), preferred_element_type=jnp.float32)
        return (summed / attn_total).astype(jnp.bfloat16)
    per_head = lax.map(head_attention, (split_heads(latent_q), split_heads(latent_k), split_heads(latent_v)))
    attended = per_head.transpose(1, 0, 2).reshape(PATCHES, inner_width)
    projected = jnp.dot(attended, latent_out, preferred_element_type=jnp.float32)
    return (hidden + projected).astype(jnp.bfloat16)
```

```python
import math

import jax
import jax.numpy as jnp
from jax import lax
from jax.experimental import pallas as pl
from jax.experimental.pallas import tpu as pltpu
from jax.sharding import PartitionSpec as P

MESH = pl.DeviceIdType.MESH
HEAD_DIM = 128
SIDE = 4
DEPTH = 16
ROWS = 256
CAP = 30.0
EPS = 1e-05
TEMPER = 1.0 / (CAP * math.sqrt(HEAD_DIM))
BF = jnp.bfloat16
F32 = jnp.float32

CROSS, OUT1, LATENT, OUT2 = (0, 96), (96, 128), (224, 384), (608, 128)
GROUPS = (CROSS, OUT1, LATENT, OUT2, (0, ROWS))
PACKED = 736
UP = DEPTH // 2
DOWN = DEPTH - 1 - UP


def dot(a, b):
    return jnp.dot(a, b, preferred_element_type=F32)


def dot_t(a, b):
    return lax.dot_general(a, b, (((1,), (1,)), ((), ())), preferred_element_type=F32)


def capped(raw):
    return jnp.exp(CAP * jnp.tanh(raw * TEMPER))


def kernel(
    bs_hbm, bp_ref, cq, ck, cv, co, gain, lq, lk, lv, lo,
    out_ref,
    bs, wp, wx, wf, pooled, kk, vv, wbuf, e1b, xbuf, rsend, rrecv, ag, acc, sq, e2, qs, kvb, oacc, lacc, att, latent, fin_s, fin_r,
    bs_sem, p1s, p1r, p2s, p2r, rls, rlr, rss, rsr, ags, agr, es, er,
):
    seq, z = lax.axis_index("seq"), lax.axis_index("tensor")
    k, c = lax.rem(seq, 2), lax.div(seq, 2)
    x, y = lax.div(c, SIDE), lax.rem(c, SIDE)
    started = []

    def wrap(i, n):
        return lax.rem(i + n, n)

    def dev(px, py, core, depth):
        return ((px * SIDE + py) * 2 + core, depth)

    def remote(src, dst, ssem, rsem, target):
        return pltpu.make_async_remote_copy(
            src_ref=src, dst_ref=dst, send_sem=ssem, recv_sem=rsem, device_id=target, device_id_type=MESH
        )

    def send(src, dst, ssem, rsem, target):
        copy = remote(src, dst, ssem, rsem, target)
        copy.start()
        started.append(copy)

    def arrive(dst, ssem, rsem):
        remote(dst, dst, ssem, rsem, partner).wait_recv()

    partner = (seq + 1 - 2 * k, z)
    up, down = (seq, wrap(z + 1, DEPTH)), (seq, wrap(z - 1, DEPTH))

    def along(half, phase, d):
        if (half == 0) == (phase == 1):
            return dev(wrap(x + d, SIDE), y, k, z)
        return dev(x, wrap(y + d, SIDE), k, z)

    def piece(buf, half, phase, d, r, n):
        part = pl.ds(r, n)
        if half == 0:
            return buf.at[wrap(x + d, SIDE), y, part, :] if phase == 1 else buf.at[:, wrap(y + d, SIDE), part, :]
        return buf.at[x, wrap(y + d, SIDE), part, :] if phase == 1 else buf.at[wrap(x + d, SIDE), :, part, :]

    def span(g, half):
        r, n = GROUPS[g]
        return r + half * (n // 2), n // 2

    def phase_start(buf, g, phase, steps):
        ssem, rsem = (p1s, p1r) if phase == 1 else (p2s, p2r)
        for half in range(2):
            own = piece(buf, half, phase, 0, *span(g, half))
            for d in steps:
                send(own, own, ssem.at[g, half, d - 1], rsem.at[g, half, d - 1], along(half, phase, d))

    def phase_wait(buf, g, phase, steps):
        ssem, rsem = (p1s, p1r) if phase == 1 else (p2s, p2r)
        for half in range(2):
            for d in steps:
                arrive(piece(buf, half, phase, -d, *span(g, half)), ssem.at[g, half, d - 1], rsem.at[g, half, d - 1])

    def relay_start(buf, g):
        for half in range(2):
            r, n = span(g, half)
            for side, d in ((0, 1), (1, 3)):
                arrive(piece(buf, half, 2, -d, r, n), p2s.at[g, half, d - 1], p2r.at[g, half, d - 1])
                part = piece(buf, half, 2, -d, r + side * (n // 2), n // 2)
                send(part, part, rls.at[g, half, side], rlr.at[g, half, side], along(half, 2, d))

    def relay_wait(buf, g):
        for half in range(2):
            r, n = span(g, half)
            for side in range(2):
                arrive(piece(buf, half, 2, 2, r + side * (n // 2), n // 2), rls.at[g, half, side], rlr.at[g, half, side])

    load = pltpu.make_async_copy(bs_hbm, bs, bs_sem)
    load.start()
    wp[x, y, 0:32, :] = cq[...]
    wp[x, y, 32:64, :] = ck[...]
    wp[x, y, 64:96, :] = cv[...]
    wp[x, y, 96:224, 0:128] = co[0:128, :]
    wp[x, y, 96:224, 128:256] = co[128:256, :]
    wp[x, y, 224:352, :] = lq[...]
    wp[x, y, 352:480, :] = lk[...]
    wp[x, y, 480:608, :] = lv[...]
    wp[x, y, 608:736, 0:128] = lo[0:128, :]
    wp[x, y, 608:736, 128:256] = lo[128:256, :]

    barrier = pltpu.get_barrier_semaphore()
    beside = [wrap(c + 1, SIDE * SIDE), wrap(c - 1, SIDE * SIDE)]
    peers = [dev(wrap(x + d, SIDE), y, k, z) for d in (1, 2, 3)]
    peers += [dev(x, wrap(y + d, SIDE), k, z) for d in (1, 2, 3)]
    peers += [partner, up, down]
    peers += [(chip * 2 + core, z) for chip in beside for core in (0, 1)]
    for peer in peers:
        pl.semaphore_signal(barrier, inc=1, device_id=peer, device_id_type=MESH)
    pl.semaphore_wait(barrier, len(peers))

    phase_start(wp, 0, 1, (1, 2, 3))

    slot_row = bp_ref[...] - (seq * 128 - 64)
    load.wait()

    def slots(first, count):
        at = lax.broadcasted_iota(jnp.int32, (count, bp_ref.shape[1]), 0) + first
        return at == slot_row

    @pl.loop(0, 4)
    def _(i):
        first = pl.multiple_of(i * 64, 64)
        mask = slots(first, 64)
        ones = mask.astype(F32)
        count = jnp.maximum(jnp.sum(ones, axis=1, keepdims=True), 1.0)
        pooled[pl.ds(first, 64), :] = (dot(ones.astype(BF), bs[...]) / count).astype(BF)

    phase_wait(wp, 0, 1, (1, 2, 3))
    phase_start(wp, 0, 2, (1, 2, 3))
    for g in (1, 2, 3):
        phase_start(wp, g, 1, (1, 2, 3))
    phase_wait(wp, 0, 2, (1, 2, 3))
    cross_part = wp.at[:, :, pl.ds(0, 96), :]
    send(cross_part, wx, es.at[0], er.at[0], partner)
    for g in (1, 2, 3):
        phase_wait(wp, g, 1, (1, 2, 3))
        phase_start(wp, g, 2, (1, 3))
    own_at, other_at = k * 32, 32 - k * 32

    def fill(source, offset):
        @pl.loop(0, SIDE * SIDE)
        def _(chip):
            px, py = lax.div(chip, SIDE), lax.rem(chip, SIDE)
            at = pl.multiple_of(chip * 64 + offset, 32)
            for m in range(3):
                wf[m, pl.ds(at, 32), :] = source[px, py, m * 32 : (m + 1) * 32, :]

    fill(wp, own_at)
    arrive(wx, es.at[0], er.at[0])
    fill(wx, other_at)

    @pl.loop(0, 4)
    def _(i):
        part = pl.ds(pl.multiple_of(i * 256, 256), 256)
        kk[part, :] = dot(bs[part, :], wf[1]).astype(BF)
        vv[part, :] = dot(bs[part, :], wf[2]).astype(BF)

    @pl.loop(0, 4)
    def _(i):
        first = pl.multiple_of(i * 64, 64)
        part = pl.ds(first, 64)
        mask = slots(first, 64)
        query = dot(pooled[part, :], wf[0]).astype(BF)
        for h in range(2):
            cols = slice(h * 128, (h + 1) * 128)
            weight = jnp.where(mask, capped(dot_t(query[:, cols], kk[:, cols])), 0.0)
            total = jnp.sum(weight, axis=1, keepdims=True)
            total = jnp.where(total > 0.0, total, 1.0)
            wbuf[k, part, cols] = (dot(weight.astype(BF), vv[:, cols]) / total).astype(BF)

    send(wbuf.at[k], wbuf.at[k], es.at[1], er.at[1], partner)
    near = wrap(c + 2 * k - 1, SIDE * SIDE)
    edge = wbuf.at[k, pl.ds(pl.multiple_of(k * 192, 64), 64), :]
    for core in (0, 1):
        send(edge, e1b.at[1 - k], es.at[2 + core], er.at[3 - k], (near * 2 + core, z))
    relay_start(wp, 1)
    arrive(wbuf.at[1 - k], es.at[1], er.at[1])
    arrive(e1b.at[0], es.at[2], er.at[2])
    arrive(e1b.at[1], es.at[3], er.at[3])
    xbuf[0:64, :] = wbuf[0, 64:128, :] + e1b[0]
    xbuf[64:192, :] = wbuf[0, 128:256, :] + wbuf[1, 0:128, :]
    xbuf[192:256, :] = wbuf[1, 128:192, :] + e1b[1]
    relay_wait(wp, 1)

    def chunk_of(g, j):
        r, n = GROUPS[g]
        return wp[lax.div(j, SIDE), lax.rem(j, SIDE), r : r + n, :]

    def reduce_depth(w, part, hook):
        for u in range(UP):
            moves = [(u, wrap(z + UP - u, DEPTH), up)]
            if u < DOWN:
                moves.append((UP + u, wrap(z - DOWN + u, DEPTH), down))
            terms = [part(j) for _, j, _ in moves]
            for (slot, _, target), term in zip(moves, terms):
                if u:
                    arrive(rrecv.at[w, slot - 1], rss.at[w, slot - 1], rsr.at[w, slot - 1])
                    term = term + rrecv[w, slot - 1].astype(F32)
                rsend[w, slot] = term.astype(BF)
                send(rsend.at[w, slot], rrecv.at[w, slot], rss.at[w, slot], rsr.at[w, slot], target)
            hook(u)
        term = part(z)
        for slot in (DEPTH - 2, UP - 1):
            arrive(rrecv.at[w, slot], rss.at[w, slot], rsr.at[w, slot])
            term = term + rrecv[w, slot].astype(F32)
        return term

    def first_part(j):
        w = chunk_of(1, j)
        return dot(xbuf[:, 0:128], w[:, 0:128]) + dot(xbuf[:, 128:256], w[:, 128:256])

    def first_hook(u):
        if u == 4:
            relay_start(wp, 2)

    latent[...] = reduce_depth(0, first_part, first_hook).astype(BF)
    ag[z] = latent[...]

    def forward(u):
        moves = [(u, wrap(z - u, DEPTH), up)]
        if u < DOWN:
            moves.append((UP + u, wrap(z + u, DEPTH), down))
        for slot, j, target in moves:
            send(ag.at[j], ag.at[j], ags.at[slot], agr.at[slot], target)

    def project(js, fresh):
        pieces, weights = [], []
        squares = None
        for j in js:
            held = ag[j].astype(F32)
            squares = held * held if squares is None else squares + held * held
            pieces.append((held * gain[pl.ds(2 * j + k, 1), :]).astype(BF))
            weights.append(chunk_of(2, j))
        left = pieces[0] if len(js) == 1 else jnp.concatenate(pieces, axis=1)
        sq[...] = squares if fresh else sq[...] + squares
        for m in range(3):
            rows = [w[m * 128 : (m + 1) * 128, :] for w in weights]
            right = rows[0] if len(js) == 1 else jnp.concatenate(rows, axis=0)
            term = dot(left, right)
            for h in range(2):
                at = (h, slice(None), slice(m * 128, (m + 1) * 128))
                piece_of = term[:, h * 128 : (h + 1) * 128]
                acc[at] = piece_of if fresh else acc[at] + piece_of

    forward(0)
    relay_wait(wp, 2)
    project([z], True)
    relay_start(wp, 3)
    for u in range(UP):
        slots_now = [(u, wrap(z - 1 - u, DEPTH))]
        if u < DOWN:
            slots_now.append((UP + u, wrap(z + 1 + u, DEPTH)))
        for slot, j in slots_now:
            arrive(ag.at[j], ags.at[slot], agr.at[slot])
        if u + 1 < UP:
            forward(u + 1)
        project([j for _, j in slots_now], False)

    acc[1 - k, :, 384:512] = sq[...]
    send(acc.at[1 - k], e2, es.at[4], er.at[4], partner)
    arrive(e2, es.at[4], er.at[4])
    mean = jnp.sum(sq[...] + e2[:, 384:512], axis=1, keepdims=True) / (2 * DEPTH * 128)
    factor = lax.rsqrt(mean + EPS)

    def joined(m):
        cols = slice(m * 128, (m + 1) * 128)
        return ((acc[k, :, cols] + e2[:, cols]) * factor).astype(BF)

    kvb[x, y, :, 0:128] = joined(1)
    kvb[x, y, :, 128:256] = joined(2)
    phase_start(kvb, 4, 1, (1, 2, 3))
    qs[...] = joined(0)

    def attend(px, py, diagonal):
        keys, values = kvb[px, py, :, 0:128], kvb[px, py, :, 128:256]
        weight = capped(dot_t(qs[...], keys))
        if diagonal:
            shape = (ROWS, ROWS)
            seen = lax.broadcasted_iota(jnp.int32, shape, 1) <= lax.broadcasted_iota(jnp.int32, shape, 0)
            weight = jnp.where(seen, weight, 0.0)
        total = weight[:, 0:128] + weight[:, 128:256]
        value = dot(weight.astype(BF), values)
        oacc[...] = value if diagonal else oacc[...] + value
        lacc[...] = total if diagonal else lacc[...] + total

    attend(x, y, True)
    phase_wait(kvb, 4, 1, (1, 2, 3))
    phase_start(kvb, 4, 2, (1, 3))
    relay_start(kvb, 4)
    relay_wait(wp, 3)
    relay_wait(kvb, 4)

    @pl.loop(0, c)
    def _(chip):
        attend(lax.div(chip, SIDE), lax.rem(chip, SIDE), False)

    total = jnp.sum(lacc[...], axis=1, keepdims=True)
    att[k] = (oacc[...] / total).astype(BF)
    send(att.at[k], att.at[k], es.at[5], er.at[5], partner)
    arrive(att.at[1 - k], es.at[5], er.at[5])

    def second_part(j):
        w = chunk_of(3, j)
        return dot(att[0], w[:, 0:128]) + dot(att[1], w[:, 128:256])

    mixed = reduce_depth(1, second_part, lambda u: None)
    fin_s[...] = (latent[...].astype(F32) + mixed).astype(BF)
    theirs = fin_s.at[pl.ds(pl.multiple_of((1 - k) * 128, 128), 128), :]
    send(theirs, fin_r, es.at[6], er.at[6], partner)
    mine = pl.ds(pl.multiple_of(k * 128, 128), 128)
    out_ref[:, mine] = fin_s[mine, :]
    arrive(fin_r, es.at[6], er.at[6])
    out_ref[:, pl.ds(pl.multiple_of((1 - k) * 128, 128), 128)] = fin_r[...]
    for copy in started:
        copy.wait_send()


def per_device(
    byte_states, byte_patch, patch_len, cross_query, cross_key, cross_value, cross_out, norm_gain,
    latent_query, latent_key, latent_value, latent_out,
):
    vmem = pl.BlockSpec(memory_space=pltpu.VMEM)
    bytes_here, width = byte_states.shape
    dma = pltpu.SemaphoreType.DMA
    groups = len(GROUPS)
    block = (ROWS, HEAD_DIM)
    return pl.pallas_call(
        kernel,
        out_shape=jax.ShapeDtypeStruct((128, 256), BF),
        in_specs=[pl.BlockSpec(memory_space=pl.ANY)] + [vmem] * 10,
        out_specs=vmem,
        scratch_shapes=[
            pltpu.VMEM((bytes_here, width), BF),
            pltpu.VMEM((SIDE, SIDE, PACKED, 256), BF),
            pltpu.VMEM((SIDE, SIDE, 96, 256), BF),
            pltpu.VMEM((3, width, 256), BF),
            pltpu.VMEM((ROWS, width), BF),
            pltpu.VMEM((bytes_here, 256), BF),
            pltpu.VMEM((bytes_here, 256), BF),
            pltpu.VMEM((2, ROWS, 256), BF),
            pltpu.VMEM((2, 64, 256), BF),
            pltpu.VMEM((ROWS, 256), BF),
            pltpu.VMEM((2, DEPTH - 1) + block, BF),
            pltpu.VMEM((2, DEPTH - 1) + block, BF),
            pltpu.VMEM((DEPTH,) + block, BF),
            pltpu.VMEM((2, ROWS, 512), F32),
            pltpu.VMEM(block, F32),
            pltpu.VMEM((ROWS, 512), F32),
            pltpu.VMEM(block, BF),
            pltpu.VMEM((SIDE, SIDE, ROWS, 256), BF),
            pltpu.VMEM(block, F32),
            pltpu.VMEM(block, F32),
            pltpu.VMEM((2,) + block, BF),
            pltpu.VMEM(block, BF),
            pltpu.VMEM(block, BF),
            pltpu.VMEM((128, HEAD_DIM), BF),
            dma,
            dma((groups, 2, 3)),
            dma((groups, 2, 3)),
            dma((groups, 2, 3)),
            dma((groups, 2, 3)),
            dma((groups, 2, 2)),
            dma((groups, 2, 2)),
            dma((2, DEPTH - 1)),
            dma((2, DEPTH - 1)),
            dma((DEPTH - 1,)),
            dma((DEPTH - 1,)),
            dma((7,)),
            dma((7,)),
        ],
        compiler_params=pltpu.CompilerParams(
            collective_id=0, has_side_effects=True, vmem_limit_bytes=60 * 1024 * 1024
        ),
        name="patches",
    )(
        byte_states, byte_patch.reshape(1, -1), cross_query, cross_key, cross_value, cross_out,
        norm_gain.reshape(-1, HEAD_DIM), latent_query, latent_key, latent_value, latent_out,
    )


def solution(mesh):
    return jax.shard_map(
        per_device,
        mesh=mesh,
        in_specs=(
            P("seq", None), P("seq"), P(), P("seq", "tensor"), P("seq", "tensor"), P("seq", "tensor"),
            P("tensor", "seq"), P(), P("seq", "tensor"), P("seq", "tensor"), P("seq", "tensor"), P("tensor", "seq"),
        ),
        out_specs=P("seq", "tensor"),
        check_vma=False,
    )
```

```python
import math

import jax
import jax.numpy as jnp
from jax import lax
from jax.experimental import pallas as pl
from jax.experimental.pallas import tpu as pltpu
from jax.sharding import PartitionSpec as P

MESH = pl.DeviceIdType.MESH
HEAD_DIM = 128
SIDE = 4
DEPTH = 16
ROWS = 256
CAP = 30.0
EPS = 1e-05
TEMPER = 1.0 / (CAP * math.sqrt(HEAD_DIM))
BF = jnp.bfloat16
F32 = jnp.float32

GROUPS = ((0, 32), (0, 128), (128, 384), (512, 128), (0, ROWS))
PACKED = 640
HOPS = DEPTH // 4
PARTS = 2
STRIP = ROWS // PARTS
PLACE = (slice(384, 512), slice(0, 128), slice(128, 256), slice(256, 384))


def dot(a, b):
    return jnp.dot(a, b, preferred_element_type=F32)


def dot_t(a, b):
    return lax.dot_general(a, b, (((1,), (1,)), ((), ())), preferred_element_type=F32)


def capped(raw):
    return jnp.exp(CAP * jnp.tanh(raw * TEMPER))


def kernel(
    bs_hbm, bp_ref, cq, ck, cv, co, gain, lq, lk, lv, lo,
    out_ref,
    bs, wp, wc, pooled, onehot, wbuf, e1b, xbuf, rsend, rrecv, ag, acc, sq, e2, qs, kvb, oacc, lacc, att, latent, fin_s, fin_r,
    bs_sem, p1s, p1r, p2s, p2r, rls, rlr, rss, rsr, ags, agr, es, er, kvs, kvr,
):
    seq, z = lax.axis_index("seq"), lax.axis_index("tensor")
    k, c = lax.rem(seq, 2), lax.div(seq, 2)
    x, y = lax.div(c, SIDE), lax.rem(c, SIDE)
    started = []

    def wrap(i, n):
        return lax.rem(i + n, n)

    def dev(px, py, core, depth):
        return ((px * SIDE + py) * 2 + core, depth)

    def remote(src, dst, ssem, rsem, target):
        return pltpu.make_async_remote_copy(
            src_ref=src, dst_ref=dst, send_sem=ssem, recv_sem=rsem, device_id=target, device_id_type=MESH
        )

    def send(src, dst, ssem, rsem, target):
        copy = remote(src, dst, ssem, rsem, target)
        copy.start()
        started.append(copy)

    def arrive(dst, ssem, rsem):
        remote(dst, dst, ssem, rsem, partner).wait_recv()

    partner = (seq + 1 - 2 * k, z)
    up, down = (seq, wrap(z + 1, DEPTH)), (seq, wrap(z - 1, DEPTH))
    above, below = (seq, wrap(z + 2, DEPTH)), (seq, wrap(z - 2, DEPTH))

    def along(half, phase, d):
        if (half == 0) == (phase == 1):
            return dev(wrap(x + d, SIDE), y, k, z)
        return dev(x, wrap(y + d, SIDE), k, z)

    def piece(buf, half, phase, d, r, n):
        part = pl.ds(r, n)
        if buf is wc:
            if half == 0:
                across = wrap(x + d, SIDE) if phase == 1 else slice(None)
                return wc.at[across, y if phase == 1 else wrap(y + d, SIDE), k, :, part, :]
            across = slice(None) if phase == 2 else wrap(y + d, SIDE)
            return wc.at[x if phase == 1 else wrap(x + d, SIDE), across, k, :, part, :]
        if half == 0:
            return buf.at[wrap(x + d, SIDE), y, part, :] if phase == 1 else buf.at[:, wrap(y + d, SIDE), part, :]
        return buf.at[x, wrap(y + d, SIDE), part, :] if phase == 1 else buf.at[wrap(x + d, SIDE), :, part, :]

    def span(g, half):
        r, n = GROUPS[g]
        return r + half * (n // 2), n // 2

    def phase_start(buf, g, phase, steps):
        ssem, rsem = (p1s, p1r) if phase == 1 else (p2s, p2r)
        for half in range(2):
            own = piece(buf, half, phase, 0, *span(g, half))
            for d in steps:
                send(own, own, ssem.at[g, half, d - 1], rsem.at[g, half, d - 1], along(half, phase, d))

    def phase_wait(buf, g, phase, steps):
        ssem, rsem = (p1s, p1r) if phase == 1 else (p2s, p2r)
        for half in range(2):
            for d in steps:
                arrive(piece(buf, half, phase, -d, *span(g, half)), ssem.at[g, half, d - 1], rsem.at[g, half, d - 1])

    def relay_start(buf, g):
        for half in range(2):
            r, n = span(g, half)
            for side, d in ((0, 1), (1, 3)):
                arrive(piece(buf, half, 2, -d, r, n), p2s.at[g, half, d - 1], p2r.at[g, half, d - 1])
                part = piece(buf, half, 2, -d, r + side * (n // 2), n // 2)
                send(part, part, rls.at[g, half, side], rlr.at[g, half, side], along(half, 2, d))

    def relay_wait(buf, g):
        for half in range(2):
            r, n = span(g, half)
            for side in range(2):
                arrive(piece(buf, half, 2, 2, r + side * (n // 2), n // 2), rls.at[g, half, side], rlr.at[g, half, side])

    load = pltpu.make_async_copy(bs_hbm, bs, bs_sem)
    load.start()
    for m, shard in enumerate((cq, ck, cv)):
        wc[x, y, k, m] = shard[...]
    for r, shard in ((0, co), (512, lo)):
        wp[x, y, r : r + 128, 0:128] = shard[0:128, :]
        wp[x, y, r : r + 128, 128:256] = shard[128:256, :]
    for m, shard in enumerate((lq, lk, lv)):
        wp[x, y, 128 * (m + 1) : 128 * (m + 2), :] = shard[...]

    barrier = pltpu.get_barrier_semaphore()
    beside = [wrap(c + 1, SIDE * SIDE), wrap(c - 1, SIDE * SIDE)]
    peers = [dev(wrap(x + d, SIDE), y, k, z) for d in (1, 2, 3)]
    peers += [dev(x, wrap(y + d, SIDE), k, z) for d in (1, 2, 3)]
    peers += [partner, up, down, above, below]
    peers += [(chip * 2 + core, z) for chip in beside for core in (0, 1)]
    for peer in peers:
        pl.semaphore_signal(barrier, inc=1, device_id=peer, device_id_type=MESH)
    slot_row = bp_ref[...] - (seq * 128 - 64)

    def slots(first, count):
        shape = (ROWS, count)
        return lax.broadcasted_iota(jnp.int32, shape, 0) == slot_row[:, first : first + count]

    ones = slots(0, bs.shape[0]).astype(F32)
    count = jnp.maximum(jnp.sum(ones, axis=1, keepdims=True), 1.0)
    onehot[...] = ones.astype(BF)
    load.wait()

    @pl.loop(0, 4)
    def _(i):
        cols = pl.ds(pl.multiple_of(i * 256, 256), 256)
        pooled[:, cols] = (dot(onehot[...], bs[:, cols]) / count).astype(BF)

    pl.semaphore_wait(barrier, len(peers))

    phase_start(wc, 0, 1, (1, 2, 3))
    phase_start(wp, 1, 1, (1, 2, 3))

    def hand_over(half, d):
        held = piece(wc, half, 2, -d, *span(0, half))
        send(held, held, es.at[7 + 4 * half + d], er.at[7 + 4 * half + d], partner)

    phase_wait(wc, 0, 1, (1, 2, 3))
    phase_start(wc, 0, 2, (1, 3, 2))
    for half in range(2):
        hand_over(half, 0)
    phase_wait(wp, 1, 1, (1, 2, 3))
    phase_start(wp, 1, 2, (1, 3))
    for d in (1, 3, 2):
        phase_wait(wc, 0, 2, (d,))
        for half in range(2):
            hand_over(half, d)
    relay_start(wp, 1)
    phase_start(wp, 2, 1, (1, 2, 3))
    for half in range(2):
        for d in range(SIDE):
            rows = pl.ds(*span(0, half))
            if half == 0:
                theirs = wc.at[:, wrap(y - d, SIDE), 1 - k, :, rows, :]
            else:
                theirs = wc.at[wrap(x - d, SIDE), :, 1 - k, :, rows, :]
            arrive(theirs, es.at[7 + 4 * half + d], er.at[7 + 4 * half + d])

    def cross(m):
        return wc[:, :, :, m].reshape(bs.shape[1], 256)

    query = dot(pooled[...], cross(0)).astype(BF)
    heads, totals = [0.0, 0.0], [0.0, 0.0]
    for i in range(4):
        part = slice(i * 256, (i + 1) * 256)
        key = dot(bs[part, :], cross(1)).astype(BF)
        value = dot(bs[part, :], cross(2)).astype(BF)
        mask = slots(i * 256, 256)
        for h in range(2):
            cols = slice(h * 128, (h + 1) * 128)
            weight = jnp.where(mask, capped(dot_t(query[:, cols], key[:, cols])), 0.0)
            totals[h] = totals[h] + weight[:, 0:128] + weight[:, 128:256]
            heads[h] = heads[h] + dot(weight.astype(BF), value[:, cols])
    for h in range(2):
        total = jnp.sum(totals[h], axis=1, keepdims=True)
        total = jnp.where(total > 0.0, total, 1.0)
        wbuf[k, :, h * 128 : (h + 1) * 128] = (heads[h] / total).astype(BF)

    send(wbuf.at[k], wbuf.at[k], es.at[1], er.at[1], partner)
    near = wrap(c + 2 * k - 1, SIDE * SIDE)
    edge = wbuf.at[k, pl.ds(pl.multiple_of(k * 192, 64), 64), :]
    for core in (0, 1):
        send(edge, e1b.at[1 - k], es.at[2 + core], er.at[3 - k], (near * 2 + core, z))
    phase_wait(wp, 2, 1, (1, 2, 3))
    phase_start(wp, 2, 2, (1, 3))
    phase_start(wp, 3, 1, (1, 2, 3))
    arrive(wbuf.at[1 - k], es.at[1], er.at[1])
    arrive(e1b.at[0], es.at[2], er.at[2])
    arrive(e1b.at[1], es.at[3], er.at[3])
    xbuf[0:64, :] = wbuf[0, 64:128, :] + e1b[0]
    xbuf[64:192, :] = wbuf[0, 128:256, :] + wbuf[1, 0:128, :]
    xbuf[192:256, :] = wbuf[1, 128:192, :] + e1b[1]
    relay_wait(wp, 1)

    def chunk_of(g, j):
        r, n = GROUPS[g]
        return wp[lax.div(j, SIDE), lax.rem(j, SIDE), r : r + n, :]

    def main_slot(side, m):
        return m if side == 0 else 2 * HOPS + m - 1

    def side_slot(side, m):
        return HOPS + m if side == 0 else 3 * HOPS - 1 + m

    def received(w, slot, p):
        rows = slice(p * STRIP, (p + 1) * STRIP)
        arrive(rrecv.at[w, slot, rows], rss.at[w, slot, p], rsr.at[w, slot, p])
        return rrecv[w, slot, rows].astype(F32)

    def give(w, slot, p, value, target):
        rows = slice(p * STRIP, (p + 1) * STRIP)
        rsend[w, slot, rows] = value.astype(BF)
        send(rsend.at[w, slot, rows], rrecv.at[w, slot, rows], rss.at[w, slot, p], rsr.at[w, slot, p], target)

    def reduce_depth(w, part, hook, result):
        def share(side, away):
            return part(wrap(z + away if side == 0 else z - away, DEPTH))

        def strips(term):
            return [term[p * STRIP : (p + 1) * STRIP] for p in range(PARTS)]

        far, near = (above, below), (up, down)
        for p, strip in enumerate(strips(share(0, 2 * HOPS))):
            give(w, main_slot(0, 0), p, strip, far[0])
        for m in range(HOPS):
            for side in range(2):
                for p, strip in enumerate(strips(share(side, 2 * HOPS - 1 - 2 * m))):
                    give(w, side_slot(side, m), p, strip, near[side])
            away = 2 * (HOPS - 1 - m)
            terms = [strips(share(side, away)) for side in range(2 if m + 1 < HOPS else 1)]
            for p in range(PARTS):
                sums = []
                for side in range(2):
                    held = received(w, side_slot(side, m), p)
                    if side == 0 or m > 0:
                        held = held + received(w, main_slot(side, m), p)
                    sums.append(held)
                if m + 1 < HOPS:
                    for side in range(2):
                        give(w, main_slot(side, m + 1), p, terms[side][p] + sums[side], far[side])
                else:
                    result(slice(p * STRIP, (p + 1) * STRIP), terms[0][p] + sums[0] + sums[1])
            hook(m)

    def first_part(j):
        w = chunk_of(1, j)
        return dot(xbuf[:, 0:128], w[:, 0:128]) + dot(xbuf[:, 128:256], w[:, 128:256])

    def first_hook(u):
        if u == 0:
            relay_start(wp, 2)
        if u == 1:
            phase_wait(wp, 3, 1, (1, 2, 3))
            phase_start(wp, 3, 2, (1, 3))

    def pass_on(m, p):
        part = pl.ds(p * STRIP, STRIP)
        for side, far, near in ((0, above, up), (1, below, down)):
            strip = ag.at[wrap(z - 2 * m if side == 0 else z + 2 * m, DEPTH), part]
            if side == 0 or m + 1 < HOPS:
                slot = main_slot(side, m + side)
                send(strip, strip, ags.at[slot, p], agr.at[slot, p], far)
            slot = side_slot(side, m)
            send(strip, strip, ags.at[slot, p], agr.at[slot, p], near)

    def first_result(rows, value):
        ag[z, rows] = value.astype(BF)
        latent[rows] = ag[z, rows]
        pass_on(0, rows.start // STRIP)

    reduce_depth(0, first_part, first_hook, first_result)

    def project(js, fresh):
        pieces, weights = [], []
        squares = None
        for j in js:
            held = ag[j].astype(F32)
            squares = held * held if squares is None else squares + held * held
            pieces.append((held * gain[pl.ds(2 * j + k, 1), :]).astype(BF))
            weights.append(chunk_of(2, j))
        left = pieces[0] if len(js) == 1 else jnp.concatenate(pieces, axis=1)
        sq[...] = squares if fresh else sq[...] + squares
        for m in range(3):
            rows = [w[m * 128 : (m + 1) * 128, :] for w in weights]
            right = rows[0] if len(js) == 1 else jnp.concatenate(rows, axis=0)
            term = dot(left, right)
            for h in range(2):
                at = (h, slice(None), PLACE[m])
                piece_of = term[:, h * 128 : (h + 1) * 128]
                acc[at] = piece_of if fresh else acc[at] + piece_of

    relay_wait(wp, 2)
    project([z], True)
    relay_start(wp, 3)
    def take(j, slot, p):
        arrive(ag.at[j, pl.ds(p * STRIP, STRIP)], ags.at[slot, p], agr.at[slot, p])

    for m in range(HOPS):
        mains = [(main_slot(0, m), wrap(z - 2 * (m + 1), DEPTH))]
        if m + 1 < HOPS:
            mains.append((main_slot(1, m + 1), wrap(z + 2 * (m + 1), DEPTH)))
        sides = [(side_slot(0, m), wrap(z - 1 - 2 * m, DEPTH)), (side_slot(1, m), wrap(z + 1 + 2 * m, DEPTH))]
        if m + 1 == HOPS:
            mains, sides = sides, mains
        for p in range(PARTS):
            for slot, j in mains:
                take(j, slot, p)
            if m + 1 < HOPS:
                pass_on(m + 1, p)
        if m + 1 == HOPS:
            project([j for _, j in mains], False)
        for slot, j in sides:
            for p in range(PARTS):
                take(j, slot, p)
        project([j for _, j in sides], False)
        if m + 1 < HOPS:
            project([j for _, j in mains], False)

    acc[1 - k, :, PLACE[3]] = sq[...]
    first, last = (slice(None), pl.ds(0, 384)), (slice(None), pl.ds(384, 128))
    send(acc.at[(1 - k,) + first], e2.at[first], es.at[4], er.at[4], partner)
    send(acc.at[(1 - k,) + last], e2.at[last], es.at[0], er.at[0], partner)
    arrive(e2.at[first], es.at[4], er.at[4])
    mean = jnp.sum(sq[...] + e2[:, PLACE[3]], axis=1, keepdims=True) / (2 * DEPTH * 128)
    factor = lax.rsqrt(mean + EPS)

    def joined(m):
        return ((acc[k, :, PLACE[m]] + e2[:, PLACE[m]]) * factor).astype(BF)

    kvb[x, y, :, 0:128] = joined(1)
    kvb[x, y, :, 128:256] = joined(2)

    def kv_piece(half, q, d, r, n):
        px, py = (wrap(x - q, SIDE), wrap(y - d, SIDE)) if half == 0 else (wrap(x - d, SIDE), wrap(y - q, SIDE))
        return kvb.at[px, py, pl.ds(r, n), :]

    def kv_on(q):
        for half in range(2):
            held = kv_piece(half, q, 0, *span(4, half))
            for side, d in ((0, 1), (1, 3)):
                send(held, held, kvs.at[half, side, q], kvr.at[half, side, q], along(half, 2, d))

    def kv_relay(q):
        for half in range(2):
            r, n = span(4, half)
            for side, d in ((0, 1), (1, 3)):
                arrive(kv_piece(half, q, d, r, n), kvs.at[half, side, q], kvr.at[half, side, q])
                part = kv_piece(half, q, d, r + side * (n // 2), n // 2)
                send(part, part, kvs.at[half, 2 + side, q], kvr.at[half, 2 + side, q], along(half, 2, d))

    def kv_last(q):
        for half in range(2):
            r, n = span(4, half)
            for side in range(2):
                part = kv_piece(half, q, 2, r + side * (n // 2), n // 2)
                arrive(part, kvs.at[half, 2 + side, q], kvr.at[half, 2 + side, q])

    phase_start(kvb, 4, 1, (1, 3, 2))
    kv_on(0)
    arrive(e2.at[last], es.at[0], er.at[0])
    qs[...] = joined(0)

    def attend(px, py, diagonal):
        keys, values = kvb[px, py, :, 0:128], kvb[px, py, :, 128:256]
        weight = capped(dot_t(qs[...], keys))
        if diagonal:
            shape = (ROWS, ROWS)
            seen = lax.broadcasted_iota(jnp.int32, shape, 1) <= lax.broadcasted_iota(jnp.int32, shape, 0)
            weight = jnp.where(seen, weight, 0.0)
        total = weight[:, 0:128] + weight[:, 128:256]
        value = dot(weight.astype(BF), values)
        oacc[...] = value if diagonal else oacc[...] + value
        lacc[...] = total if diagonal else lacc[...] + total

    attend(x, y, True)
    for d in (1, 3):
        phase_wait(kvb, 4, 1, (d,))
        kv_on(d)
    kv_relay(0)
    phase_wait(kvb, 4, 1, (2,))
    kv_on(2)
    for q in (1, 3, 2):
        kv_relay(q)
    relay_wait(wp, 3)
    for q in range(SIDE):
        kv_last(q)

    @pl.loop(0, c)
    def _(chip):
        attend(lax.div(chip, SIDE), lax.rem(chip, SIDE), False)

    total = jnp.sum(lacc[...], axis=1, keepdims=True)
    att[k] = (oacc[...] / total).astype(BF)
    send(att.at[k], att.at[k], es.at[5], er.at[5], partner)
    arrive(att.at[1 - k], es.at[5], er.at[5])

    def second_part(j):
        w = chunk_of(3, j)
        return dot(att[0], w[:, 0:128]) + dot(att[1], w[:, 128:256])

    def second_result(rows, value):
        fin_s[rows] = (latent[rows].astype(F32) + value).astype(BF)

    reduce_depth(1, second_part, lambda m: None, second_result)
    theirs = fin_s.at[pl.ds(pl.multiple_of((1 - k) * 128, 128), 128), :]
    send(theirs, fin_r, es.at[6], er.at[6], partner)
    mine = pl.ds(pl.multiple_of(k * 128, 128), 128)
    out_ref[:, mine] = fin_s[mine, :]
    arrive(fin_r, es.at[6], er.at[6])
    out_ref[:, pl.ds(pl.multiple_of((1 - k) * 128, 128), 128)] = fin_r[...]
    for copy in started:
        copy.wait_send()


def per_device(
    byte_states, byte_patch, patch_len, cross_query, cross_key, cross_value, cross_out, norm_gain,
    latent_query, latent_key, latent_value, latent_out,
):
    vmem = pl.BlockSpec(memory_space=pltpu.VMEM)
    bytes_here, width = byte_states.shape
    dma = pltpu.SemaphoreType.DMA
    groups = len(GROUPS)
    block = (ROWS, HEAD_DIM)
    return pl.pallas_call(
        kernel,
        out_shape=jax.ShapeDtypeStruct((128, 256), BF),
        in_specs=[pl.BlockSpec(memory_space=pl.ANY)] + [vmem] * 10,
        out_specs=vmem,
        scratch_shapes=[
            pltpu.VMEM((bytes_here, width), BF),
            pltpu.VMEM((SIDE, SIDE, PACKED, 256), BF),
            pltpu.VMEM((SIDE, SIDE, 2, 3, 32, 256), BF),
            pltpu.VMEM((ROWS, width), BF),
            pltpu.VMEM((ROWS, bytes_here), BF),
            pltpu.VMEM((2, ROWS, 256), BF),
            pltpu.VMEM((2, 64, 256), BF),
            pltpu.VMEM((ROWS, 256), BF),
            pltpu.VMEM((2, DEPTH - 1) + block, BF),
            pltpu.VMEM((2, DEPTH - 1) + block, BF),
            pltpu.VMEM((DEPTH,) + block, BF),
            pltpu.VMEM((2, ROWS, 512), F32),
            pltpu.VMEM(block, F32),
            pltpu.VMEM((ROWS, 512), F32),
            pltpu.VMEM(block, BF),
            pltpu.VMEM((SIDE, SIDE, ROWS, 256), BF),
            pltpu.VMEM(block, F32),
            pltpu.VMEM(block, F32),
            pltpu.VMEM((2,) + block, BF),
            pltpu.VMEM(block, BF),
            pltpu.VMEM(block, BF),
            pltpu.VMEM((128, HEAD_DIM), BF),
            dma,
            dma((groups, 2, 3)),
            dma((groups, 2, 3)),
            dma((groups, 2, 3)),
            dma((groups, 2, 3)),
            dma((groups, 2, 2)),
            dma((groups, 2, 2)),
            dma((2, DEPTH - 1, PARTS)),
            dma((2, DEPTH - 1, PARTS)),
            dma((DEPTH - 1, PARTS)),
            dma((DEPTH - 1, PARTS)),
            dma((15,)),
            dma((15,)),
            dma((2, SIDE, SIDE)),
            dma((2, SIDE, SIDE)),
        ],
        compiler_params=pltpu.CompilerParams(
            collective_id=0, has_side_effects=True, vmem_limit_bytes=60 * 1024 * 1024
        ),
        name="patches",
    )(
        byte_states, byte_patch.reshape(1, -1), cross_query, cross_key, cross_value, cross_out,
        norm_gain.reshape(-1, HEAD_DIM), latent_query, latent_key, latent_value, latent_out,
    )


def solution(mesh):
    return jax.shard_map(
        per_device,
        mesh=mesh,
        in_specs=(
            P("seq", None), P("seq"), P(), P("seq", "tensor"), P("seq", "tensor"), P("seq", "tensor"),
            P("tensor", "seq"), P(), P("seq", "tensor"), P("seq", "tensor"), P("seq", "tensor"), P("tensor", "seq"),
        ),
        out_specs=P("seq", "tensor"),
        check_vma=False,
    )
```

```python
import math

import jax
import jax.numpy as jnp
from jax import lax
from jax.experimental import pallas as pl
from jax.experimental.pallas import tpu as pltpu
from jax.sharding import PartitionSpec as P

MESH = pl.DeviceIdType.MESH
HEAD_DIM = 128
SIDE = 4
DEPTH = 16
ROWS = 256
CAP = 30.0
EPS = 1e-05
TEMPER = 1.0 / (CAP * math.sqrt(HEAD_DIM))
BF = jnp.bfloat16
F32 = jnp.float32

GROUPS = ((0, 32), (0, 128), (128, 384), (512, 128), (0, ROWS))
PACKED = 640
HOPS = DEPTH // 4
PARTS = 2
STRIP = ROWS // PARTS
PLACE = (slice(384, 512), slice(0, 128), slice(128, 256), slice(256, 384))


def dot(a, b):
    return jnp.dot(a, b, preferred_element_type=F32)


def dot_t(a, b):
    return lax.dot_general(a, b, (((1,), (1,)), ((), ())), preferred_element_type=F32)


def capped(raw):
    return jnp.exp(CAP * jnp.tanh(raw * TEMPER))


def kernel(
    bs_hbm, bp_ref, cq, ck, cv, co, gain, lq, lk, lv, lo,
    out_ref,
    bs, wp, wc, pooled, onehot, wbuf, e1b, xbuf, rsend, rrecv, ag, acc, sq, e2, qs, kvb, oacc, lacc, att, latent, fin_s, fin_r,
    bs_sem, p1s, p1r, p2s, p2r, rls, rlr, rss, rsr, ags, agr, es, er, kvs, kvr,
):
    seq, z = lax.axis_index("seq"), lax.axis_index("tensor")
    k, c = lax.rem(seq, 2), lax.div(seq, 2)
    x, y = lax.div(c, SIDE), lax.rem(c, SIDE)
    started = []

    def wrap(i, n):
        return lax.rem(i + n, n)

    def dev(px, py, core, depth):
        return ((px * SIDE + py) * 2 + core, depth)

    def remote(src, dst, ssem, rsem, target):
        return pltpu.make_async_remote_copy(
            src_ref=src, dst_ref=dst, send_sem=ssem, recv_sem=rsem, device_id=target, device_id_type=MESH
        )

    def send(src, dst, ssem, rsem, target):
        copy = remote(src, dst, ssem, rsem, target)
        copy.start()
        started.append(copy)

    def arrive(dst, ssem, rsem):
        remote(dst, dst, ssem, rsem, partner).wait_recv()

    partner = (seq + 1 - 2 * k, z)
    up, down = (seq, wrap(z + 1, DEPTH)), (seq, wrap(z - 1, DEPTH))
    above, below = (seq, wrap(z + 2, DEPTH)), (seq, wrap(z - 2, DEPTH))

    def along(half, phase, d):
        if (half == 0) == (phase == 1):
            return dev(wrap(x + d, SIDE), y, k, z)
        return dev(x, wrap(y + d, SIDE), k, z)

    def piece(buf, half, phase, d, r, n):
        part = pl.ds(r, n)
        if buf is wc:
            if half == 0:
                across = wrap(x + d, SIDE) if phase == 1 else slice(None)
                return wc.at[across, y if phase == 1 else wrap(y + d, SIDE), k, :, part, :]
            across = slice(None) if phase == 2 else wrap(y + d, SIDE)
            return wc.at[x if phase == 1 else wrap(x + d, SIDE), across, k, :, part, :]
        if half == 0:
            return buf.at[wrap(x + d, SIDE), y, part, :] if phase == 1 else buf.at[:, wrap(y + d, SIDE), part, :]
        return buf.at[x, wrap(y + d, SIDE), part, :] if phase == 1 else buf.at[wrap(x + d, SIDE), :, part, :]

    def span(g, half):
        r, n = GROUPS[g]
        return r + half * (n // 2), n // 2

    def phase_start(buf, g, phase, steps):
        ssem, rsem = (p1s, p1r) if phase == 1 else (p2s, p2r)
        for half in range(2):
            own = piece(buf, half, phase, 0, *span(g, half))
            for d in steps:
                send(own, own, ssem.at[g, half, d - 1], rsem.at[g, half, d - 1], along(half, phase, d))

    def phase_wait(buf, g, phase, steps):
        ssem, rsem = (p1s, p1r) if phase == 1 else (p2s, p2r)
        for half in range(2):
            for d in steps:
                arrive(piece(buf, half, phase, -d, *span(g, half)), ssem.at[g, half, d - 1], rsem.at[g, half, d - 1])

    def relay_start(buf, g):
        for half in range(2):
            r, n = span(g, half)
            for side, d in ((0, 1), (1, 3)):
                arrive(piece(buf, half, 2, -d, r, n), p2s.at[g, half, d - 1], p2r.at[g, half, d - 1])
                part = piece(buf, half, 2, -d, r + side * (n // 2), n // 2)
                send(part, part, rls.at[g, half, side], rlr.at[g, half, side], along(half, 2, d))

    def relay_wait(buf, g):
        for half in range(2):
            r, n = span(g, half)
            for side in range(2):
                arrive(piece(buf, half, 2, 2, r + side * (n // 2), n // 2), rls.at[g, half, side], rlr.at[g, half, side])

    load = pltpu.make_async_copy(bs_hbm, bs, bs_sem)
    load.start()
    for m, shard in enumerate((cq, ck, cv)):
        wc[x, y, k, m] = shard[...]
    for r, shard in ((0, co), (512, lo)):
        wp[x, y, r : r + 128, 0:128] = shard[0:128, :]
        wp[x, y, r : r + 128, 128:256] = shard[128:256, :]
    for m, shard in enumerate((lq, lk, lv)):
        wp[x, y, 128 * (m + 1) : 128 * (m + 2), :] = shard[...]

    barrier = pltpu.get_barrier_semaphore()
    beside = [wrap(c + 1, SIDE * SIDE), wrap(c - 1, SIDE * SIDE)]
    peers = [dev(wrap(x + d, SIDE), y, k, z) for d in (1, 2, 3)]
    peers += [dev(x, wrap(y + d, SIDE), k, z) for d in (1, 2, 3)]
    peers += [partner, up, down, above, below]
    peers += [(chip * 2 + core, z) for chip in beside for core in (0, 1)]
    for peer in peers:
        pl.semaphore_signal(barrier, inc=1, device_id=peer, device_id_type=MESH)
    slot_row = bp_ref[...] - (seq * 128 - 64)

    def slots(first, count):
        shape = (ROWS, count)
        return lax.broadcasted_iota(jnp.int32, shape, 0) == slot_row[:, first : first + count]

    ones = slots(0, bs.shape[0]).astype(F32)
    count = jnp.maximum(jnp.sum(ones, axis=1, keepdims=True), 1.0)
    onehot[...] = ones.astype(BF)
    load.wait()

    @pl.loop(0, 4)
    def _(i):
        cols = pl.ds(pl.multiple_of(i * 256, 256), 256)
        pooled[:, cols] = (dot(onehot[...], bs[:, cols]) / count).astype(BF)

    pl.semaphore_wait(barrier, len(peers))

    phase_start(wc, 0, 1, (1, 2, 3))
    phase_start(wp, 1, 1, (1, 2, 3))

    def hand_over(half, d):
        held = piece(wc, half, 2, -d, *span(0, half))
        send(held, held, es.at[7 + 4 * half + d], er.at[7 + 4 * half + d], partner)

    phase_wait(wc, 0, 1, (1, 2, 3))
    phase_start(wc, 0, 2, (1, 3, 2))
    for half in range(2):
        hand_over(half, 0)
    phase_wait(wp, 1, 1, (1, 2, 3))
    phase_start(wp, 1, 2, (1, 3))
    for d in (1, 3, 2):
        phase_wait(wc, 0, 2, (d,))
        for half in range(2):
            hand_over(half, d)
    relay_start(wp, 1)
    for half in range(2):
        for d in range(SIDE):
            rows = pl.ds(*span(0, half))
            if half == 0:
                theirs = wc.at[:, wrap(y - d, SIDE), 1 - k, :, rows, :]
            else:
                theirs = wc.at[wrap(x - d, SIDE), :, 1 - k, :, rows, :]
            arrive(theirs, es.at[7 + 4 * half + d], er.at[7 + 4 * half + d])

    def cross(m):
        return wc[:, :, :, m].reshape(bs.shape[1], 256)

    query = dot(pooled[...], cross(0)).astype(BF)
    heads, totals = [0.0, 0.0], [0.0, 0.0]
    for i in range(4):
        part = slice(i * 256, (i + 1) * 256)
        key = dot(bs[part, :], cross(1)).astype(BF)
        value = dot(bs[part, :], cross(2)).astype(BF)
        mask = slots(i * 256, 256)
        for h in range(2):
            cols = slice(h * 128, (h + 1) * 128)
            weight = jnp.where(mask, capped(dot_t(query[:, cols], key[:, cols])), 0.0)
            totals[h] = totals[h] + weight[:, 0:128] + weight[:, 128:256]
            heads[h] = heads[h] + dot(weight.astype(BF), value[:, cols])
    for h in range(2):
        total = jnp.sum(totals[h], axis=1, keepdims=True)
        total = jnp.where(total > 0.0, total, 1.0)
        wbuf[k, :, h * 128 : (h + 1) * 128] = (heads[h] / total).astype(BF)

    send(wbuf.at[k], wbuf.at[k], es.at[1], er.at[1], partner)
    near = wrap(c + 2 * k - 1, SIDE * SIDE)
    edge = wbuf.at[k, pl.ds(pl.multiple_of(k * 192, 64), 64), :]
    for core in (0, 1):
        send(edge, e1b.at[1 - k], es.at[2 + core], er.at[3 - k], (near * 2 + core, z))
    phase_start(wp, 2, 1, (1, 3, 2))
    arrive(wbuf.at[1 - k], es.at[1], er.at[1])
    arrive(e1b.at[0], es.at[2], er.at[2])
    arrive(e1b.at[1], es.at[3], er.at[3])
    xbuf[0:64, :] = wbuf[0, 64:128, :] + e1b[0]
    xbuf[64:192, :] = wbuf[0, 128:256, :] + wbuf[1, 0:128, :]
    xbuf[192:256, :] = wbuf[1, 128:192, :] + e1b[1]
    relay_wait(wp, 1)

    def chunk_of(g, j):
        r, n = GROUPS[g]
        return wp[lax.div(j, SIDE), lax.rem(j, SIDE), r : r + n, :]

    def main_slot(side, m):
        return m if side == 0 else 2 * HOPS + m - 1

    def side_slot(side, m):
        return HOPS + m if side == 0 else 3 * HOPS - 1 + m

    def received(w, slot, p):
        rows = slice(p * STRIP, (p + 1) * STRIP)
        arrive(rrecv.at[w, slot, rows], rss.at[w, slot, p], rsr.at[w, slot, p])
        return rrecv[w, slot, rows].astype(F32)

    def give(w, slot, p, value, target):
        rows = slice(p * STRIP, (p + 1) * STRIP)
        rsend[w, slot, rows] = value.astype(BF)
        send(rsend.at[w, slot, rows], rrecv.at[w, slot, rows], rss.at[w, slot, p], rsr.at[w, slot, p], target)

    def reduce_depth(w, part, hook, result):
        def share(side, away):
            return part(wrap(z + away if side == 0 else z - away, DEPTH))

        def strips(term):
            return [term[p * STRIP : (p + 1) * STRIP] for p in range(PARTS)]

        far, near = (above, below), (up, down)

        def give_step(m, p, mains, sides):
            for side, main in mains.items():
                give(w, main_slot(side, m), p, main, far[side])
            for side in range(2):
                give(w, side_slot(side, m), p, sides[side][p], near[side])

        first_main = strips(share(0, 2 * HOPS))
        first_sides = [strips(share(side, 2 * HOPS - 1)) for side in range(2)]
        give_step(0, 0, {0: first_main[0]}, first_sides)
        early = [received(w, side_slot(side, 0), 0) for side in range(2)]
        give_step(0, 1, {0: first_main[1]}, first_sides)
        for m in range(HOPS):
            last = m + 1 == HOPS
            away = 2 * (HOPS - 1 - m)
            terms = [strips(share(side, away)) for side in range(1 if last else 2)]
            sides = None if last else [strips(share(side, away - 1)) for side in range(2)]
            for p in range(PARTS):
                sums = early if (m, p) == (0, 0) else [received(w, side_slot(side, m), p) for side in range(2)]
                for side in range(2 if m else 1):
                    sums[side] = sums[side] + received(w, main_slot(side, m), p)
                if last:
                    result(slice(p * STRIP, (p + 1) * STRIP), terms[0][p] + sums[0] + sums[1])
                else:
                    give_step(m + 1, p, {side: terms[side][p] + sums[side] for side in range(2)}, sides)
            hook(m)

    def first_part(j):
        w = chunk_of(1, j)
        return dot(xbuf[:, 0:128], w[:, 0:128]) + dot(xbuf[:, 128:256], w[:, 128:256])

    def first_hook(u):
        if u == 0:
            phase_wait(wp, 2, 1, (1, 2, 3))
            phase_start(wp, 2, 2, (1, 3))
        if u == 2:
            relay_start(wp, 2)
        if u == 3:
            phase_start(wp, 3, 1, (1, 2, 3))

    def pass_on(m, p):
        part = pl.ds(p * STRIP, STRIP)
        for side, far, near in ((0, above, up), (1, below, down)):
            strip = ag.at[wrap(z - 2 * m if side == 0 else z + 2 * m, DEPTH), part]
            if side == 0 or m + 1 < HOPS:
                slot = main_slot(side, m + side)
                send(strip, strip, ags.at[slot, p], agr.at[slot, p], far)
            slot = side_slot(side, m)
            send(strip, strip, ags.at[slot, p], agr.at[slot, p], near)

    def first_result(rows, value):
        ag[z, rows] = value.astype(BF)
        latent[rows] = ag[z, rows]
        pass_on(0, rows.start // STRIP)

    reduce_depth(0, first_part, first_hook, first_result)

    def project(js, fresh):
        pieces, weights = [], []
        squares = None
        for j in js:
            held = ag[j].astype(F32)
            squares = held * held if squares is None else squares + held * held
            pieces.append((held * gain[pl.ds(2 * j + k, 1), :]).astype(BF))
            weights.append(chunk_of(2, j))
        left = pieces[0] if len(js) == 1 else jnp.concatenate(pieces, axis=1)
        sq[...] = squares if fresh else sq[...] + squares
        for m in range(3):
            rows = [w[m * 128 : (m + 1) * 128, :] for w in weights]
            right = rows[0] if len(js) == 1 else jnp.concatenate(rows, axis=0)
            term = dot(left, right)
            for h in range(2):
                at = (h, slice(None), PLACE[m])
                piece_of = term[:, h * 128 : (h + 1) * 128]
                acc[at] = piece_of if fresh else acc[at] + piece_of

    relay_wait(wp, 2)
    project([z], True)
    def take(j, slot, p):
        arrive(ag.at[j, pl.ds(p * STRIP, STRIP)], ags.at[slot, p], agr.at[slot, p])

    held = None
    for m in range(HOPS):
        mains = [(main_slot(0, m), wrap(z - 2 * (m + 1), DEPTH))]
        if m + 1 < HOPS:
            mains.append((main_slot(1, m + 1), wrap(z + 2 * (m + 1), DEPTH)))
        sides = [(side_slot(0, m), wrap(z - 1 - 2 * m, DEPTH)), (side_slot(1, m), wrap(z + 1 + 2 * m, DEPTH))]
        for p in range(PARTS):
            if m + 1 == HOPS and p == 1:
                for slot, j in sides:
                    for strip in range(PARTS):
                        take(j, slot, strip)
                project([j for _, j in sides], False)
            for slot, j in mains:
                take(j, slot, p)
            if m + 1 < HOPS:
                pass_on(m + 1, p)
            if p == 0 and held is not None:
                project(held, False)
        if m + 1 < HOPS:
            for slot, j in sides:
                for p in range(PARTS):
                    take(j, slot, p)
            project([j for _, j in sides], False)
        held = [j for _, j in mains]
        if m == 1:
            phase_wait(wp, 3, 1, (1, 2, 3))
            phase_start(wp, 3, 2, (1, 3))
    project(held, False)

    acc[1 - k, :, PLACE[3]] = sq[...]
    first, last = (slice(None), pl.ds(0, 384)), (slice(None), pl.ds(384, 128))
    send(acc.at[(1 - k,) + first], e2.at[first], es.at[4], er.at[4], partner)
    send(acc.at[(1 - k,) + last], e2.at[last], es.at[0], er.at[0], partner)
    arrive(e2.at[first], es.at[4], er.at[4])
    mean = jnp.sum(sq[...] + e2[:, PLACE[3]], axis=1, keepdims=True) / (2 * DEPTH * 128)
    factor = lax.rsqrt(mean + EPS)

    def joined(m):
        return ((acc[k, :, PLACE[m]] + e2[:, PLACE[m]]) * factor).astype(BF)

    kvb[x, y, :, 0:128] = joined(1)
    kvb[x, y, :, 128:256] = joined(2)

    def kv_piece(half, q, d, r, n):
        px, py = (wrap(x - q, SIDE), wrap(y - d, SIDE)) if half == 0 else (wrap(x - d, SIDE), wrap(y - q, SIDE))
        return kvb.at[px, py, pl.ds(r, n), :]

    def kv_on(q):
        for half in range(2):
            held = kv_piece(half, q, 0, *span(4, half))
            for side, d in ((0, 1), (1, 3)):
                send(held, held, kvs.at[half, side, q], kvr.at[half, side, q], along(half, 2, d))

    def kv_relay(q):
        for half in range(2):
            r, n = span(4, half)
            for side, d in ((0, 1), (1, 3)):
                arrive(kv_piece(half, q, d, r, n), kvs.at[half, side, q], kvr.at[half, side, q])
                part = kv_piece(half, q, d, r + side * (n // 2), n // 2)
                send(part, part, kvs.at[half, 2 + side, q], kvr.at[half, 2 + side, q], along(half, 2, d))

    def kv_last(q):
        for half in range(2):
            r, n = span(4, half)
            for side in range(2):
                part = kv_piece(half, q, 2, r + side * (n // 2), n // 2)
                arrive(part, kvs.at[half, 2 + side, q], kvr.at[half, 2 + side, q])

    phase_start(kvb, 4, 1, (1, 3, 2))
    kv_on(0)
    arrive(e2.at[last], es.at[0], er.at[0])
    qs[...] = joined(0)

    def attend(blocks):
        value = total = None
        for dx, dy in blocks:
            px, py = wrap(x + dx, SIDE), wrap(y + dy, SIDE)
            weight = capped(dot_t(qs[...], kvb[px, py, :, 0:128]))
            if (dx, dy) == (0, 0):
                shape = (ROWS, ROWS)
                seen = lax.broadcasted_iota(jnp.int32, shape, 1) <= lax.broadcasted_iota(jnp.int32, shape, 0)
                weight = jnp.where(seen, weight, 0.0)
            else:
                weight = weight * jnp.where(px * SIDE + py < c, 1.0, 0.0)
            term = dot(weight.astype(BF), kvb[px, py, :, 128:256])
            mass = weight[:, 0:128] + weight[:, 128:256]
            value = term if value is None else value + term
            total = mass if total is None else total + mass
        own = blocks[0] == (0, 0)
        oacc[...] = value if own else oacc[...] + value
        lacc[...] = total if own else lacc[...] + total

    attend([(0, 0)])
    for d in (1, 3):
        phase_wait(kvb, 4, 1, (d,))
        kv_on(d)
    kv_relay(0)
    phase_wait(kvb, 4, 1, (2,))
    kv_on(2)
    attend([(1, 0), (3, 0), (0, 1), (0, 3)])
    kv_relay(1)
    kv_relay(3)
    attend([(1, 1), (1, 3), (3, 1), (3, 3)])
    kv_relay(2)
    relay_start(wp, 3)
    for q in range(SIDE):
        kv_last(q)
    attend([(2, 0), (2, 1), (2, 2), (2, 3), (0, 2), (1, 2), (3, 2)])
    relay_wait(wp, 3)

    total = jnp.sum(lacc[...], axis=1, keepdims=True)
    att[k] = (oacc[...] / total).astype(BF)
    send(att.at[k], att.at[k], es.at[5], er.at[5], partner)
    arrive(att.at[1 - k], es.at[5], er.at[5])

    def second_part(j):
        w = chunk_of(3, j)
        return dot(att[0], w[:, 0:128]) + dot(att[1], w[:, 128:256])

    def second_result(rows, value):
        fin_s[rows] = (latent[rows].astype(F32) + value).astype(BF)

    reduce_depth(1, second_part, lambda m: None, second_result)
    theirs = fin_s.at[pl.ds(pl.multiple_of((1 - k) * 128, 128), 128), :]
    send(theirs, fin_r, es.at[6], er.at[6], partner)
    mine = pl.ds(pl.multiple_of(k * 128, 128), 128)
    out_ref[:, mine] = fin_s[mine, :]
    arrive(fin_r, es.at[6], er.at[6])
    out_ref[:, pl.ds(pl.multiple_of((1 - k) * 128, 128), 128)] = fin_r[...]
    for copy in started:
        copy.wait_send()


def per_device(
    byte_states, byte_patch, patch_len, cross_query, cross_key, cross_value, cross_out, norm_gain,
    latent_query, latent_key, latent_value, latent_out,
):
    vmem = pl.BlockSpec(memory_space=pltpu.VMEM)
    bytes_here, width = byte_states.shape
    dma = pltpu.SemaphoreType.DMA
    groups = len(GROUPS)
    block = (ROWS, HEAD_DIM)
    return pl.pallas_call(
        kernel,
        out_shape=jax.ShapeDtypeStruct((128, 256), BF),
        in_specs=[pl.BlockSpec(memory_space=pl.ANY)] + [vmem] * 10,
        out_specs=vmem,
        scratch_shapes=[
            pltpu.VMEM((bytes_here, width), BF),
            pltpu.VMEM((SIDE, SIDE, PACKED, 256), BF),
            pltpu.VMEM((SIDE, SIDE, 2, 3, 32, 256), BF),
            pltpu.VMEM((ROWS, width), BF),
            pltpu.VMEM((ROWS, bytes_here), BF),
            pltpu.VMEM((2, ROWS, 256), BF),
            pltpu.VMEM((2, 64, 256), BF),
            pltpu.VMEM((ROWS, 256), BF),
            pltpu.VMEM((2, DEPTH - 1) + block, BF),
            pltpu.VMEM((2, DEPTH - 1) + block, BF),
            pltpu.VMEM((DEPTH,) + block, BF),
            pltpu.VMEM((2, ROWS, 512), F32),
            pltpu.VMEM(block, F32),
            pltpu.VMEM((ROWS, 512), F32),
            pltpu.VMEM(block, BF),
            pltpu.VMEM((SIDE, SIDE, ROWS, 256), BF),
            pltpu.VMEM(block, F32),
            pltpu.VMEM(block, F32),
            pltpu.VMEM((2,) + block, BF),
            pltpu.VMEM(block, BF),
            pltpu.VMEM(block, BF),
            pltpu.VMEM((128, HEAD_DIM), BF),
            dma,
            dma((groups, 2, 3)),
            dma((groups, 2, 3)),
            dma((groups, 2, 3)),
            dma((groups, 2, 3)),
            dma((groups, 2, 2)),
            dma((groups, 2, 2)),
            dma((2, DEPTH - 1, PARTS)),
            dma((2, DEPTH - 1, PARTS)),
            dma((DEPTH - 1, PARTS)),
            dma((DEPTH - 1, PARTS)),
            dma((15,)),
            dma((15,)),
            dma((2, SIDE, SIDE)),
            dma((2, SIDE, SIDE)),
        ],
        compiler_params=pltpu.CompilerParams(
            collective_id=0, has_side_effects=True, vmem_limit_bytes=60 * 1024 * 1024
        ),
        name="patches",
    )(
        byte_states, byte_patch.reshape(1, -1), cross_query, cross_key, cross_value, cross_out,
        norm_gain.reshape(-1, HEAD_DIM), latent_query, latent_key, latent_value, latent_out,
    )


def solution(mesh):
    return jax.shard_map(
        per_device,
        mesh=mesh,
        in_specs=(
            P("seq", None), P("seq"), P(), P("seq", "tensor"), P("seq", "tensor"), P("seq", "tensor"),
            P("tensor", "seq"), P(), P("seq", "tensor"), P("seq", "tensor"), P("seq", "tensor"), P("tensor", "seq"),
        ),
        out_specs=P("seq", "tensor"),
        check_vma=False,
    )
```

```python
import math

import jax
import jax.numpy as jnp
from jax import lax
from jax.experimental import pallas as pl
from jax.experimental.pallas import tpu as pltpu
from jax.sharding import PartitionSpec as P

MESH = pl.DeviceIdType.MESH
HEAD_DIM = 128
SIDE = 4
DEPTH = 16
ROWS = 256
CAP = 30.0
EPS = 1e-05
TEMPER = 1.0 / (CAP * math.sqrt(HEAD_DIM))
BF = jnp.bfloat16
F32 = jnp.float32

GROUPS = ((0, 32), (0, 128), (128, 384), (512, 128), (0, ROWS))
PACKED = 640
HOPS = DEPTH // 4
PARTS = 4
STRIP = ROWS // PARTS
PLACE = (slice(384, 512), slice(0, 128), slice(128, 256), slice(256, 384))


def dot(a, b):
    return jnp.dot(a, b, preferred_element_type=F32)


def dot_t(a, b):
    return lax.dot_general(a, b, (((1,), (1,)), ((), ())), preferred_element_type=F32)


def capped(raw):
    return jnp.exp(CAP * jnp.tanh(raw * TEMPER))


def kernel(
    bs_hbm, bp_ref, cq, ck, cv, co, gain, lq, lk, lv, lo,
    out_ref,
    bs, wp, wc, pooled, onehot, wbuf, e1b, xbuf, rsend, rrecv, ag, acc, sq, e2, qs, kvb, oacc, lacc, att, latent, fin_s, fin_r,
    bs_sem, p1s, p1r, p2s, p2r, rls, rlr, rss, rsr, ags, agr, es, er, kvs, kvr,
):
    seq, z = lax.axis_index("seq"), lax.axis_index("tensor")
    k, c = lax.rem(seq, 2), lax.div(seq, 2)
    x, y = lax.div(c, SIDE), lax.rem(c, SIDE)
    started = []

    def wrap(i, n):
        return lax.rem(i + n, n)

    def dev(px, py, core, depth):
        return ((px * SIDE + py) * 2 + core, depth)

    def remote(src, dst, ssem, rsem, target):
        return pltpu.make_async_remote_copy(
            src_ref=src, dst_ref=dst, send_sem=ssem, recv_sem=rsem, device_id=target, device_id_type=MESH
        )

    def send(src, dst, ssem, rsem, target):
        copy = remote(src, dst, ssem, rsem, target)
        copy.start()
        started.append(copy)

    def arrive(dst, ssem, rsem):
        remote(dst, dst, ssem, rsem, partner).wait_recv()

    partner = (seq + 1 - 2 * k, z)
    up, down = (seq, wrap(z + 1, DEPTH)), (seq, wrap(z - 1, DEPTH))
    above, below = (seq, wrap(z + 2, DEPTH)), (seq, wrap(z - 2, DEPTH))

    def along(half, phase, d):
        if (half == 0) == (phase == 1):
            return dev(wrap(x + d, SIDE), y, k, z)
        return dev(x, wrap(y + d, SIDE), k, z)

    def piece(buf, half, phase, d, r, n):
        part = pl.ds(r, n)
        if buf is wc:
            if half == 0:
                across = wrap(x + d, SIDE) if phase == 1 else slice(None)
                return wc.at[across, y if phase == 1 else wrap(y + d, SIDE), k, :, part, :]
            across = slice(None) if phase == 2 else wrap(y + d, SIDE)
            return wc.at[x if phase == 1 else wrap(x + d, SIDE), across, k, :, part, :]
        if half == 0:
            return buf.at[wrap(x + d, SIDE), y, part, :] if phase == 1 else buf.at[:, wrap(y + d, SIDE), part, :]
        return buf.at[x, wrap(y + d, SIDE), part, :] if phase == 1 else buf.at[wrap(x + d, SIDE), :, part, :]

    def span(g, half):
        r, n = GROUPS[g]
        return r + half * (n // 2), n // 2

    def phase_start(buf, g, phase, steps):
        ssem, rsem = (p1s, p1r) if phase == 1 else (p2s, p2r)
        for half in range(2):
            own = piece(buf, half, phase, 0, *span(g, half))
            for d in steps:
                send(own, own, ssem.at[g, half, d - 1], rsem.at[g, half, d - 1], along(half, phase, d))

    def phase_wait(buf, g, phase, steps):
        ssem, rsem = (p1s, p1r) if phase == 1 else (p2s, p2r)
        for half in range(2):
            for d in steps:
                arrive(piece(buf, half, phase, -d, *span(g, half)), ssem.at[g, half, d - 1], rsem.at[g, half, d - 1])

    def relay_start(buf, g):
        for half in range(2):
            r, n = span(g, half)
            for side, d in ((0, 1), (1, 3)):
                arrive(piece(buf, half, 2, -d, r, n), p2s.at[g, half, d - 1], p2r.at[g, half, d - 1])
                part = piece(buf, half, 2, -d, r + side * (n // 2), n // 2)
                send(part, part, rls.at[g, half, side], rlr.at[g, half, side], along(half, 2, d))

    def relay_wait(buf, g):
        for half in range(2):
            r, n = span(g, half)
            for side in range(2):
                arrive(piece(buf, half, 2, 2, r + side * (n // 2), n // 2), rls.at[g, half, side], rlr.at[g, half, side])

    load = pltpu.make_async_copy(bs_hbm, bs, bs_sem)
    load.start()
    for m, shard in enumerate((cq, ck, cv)):
        wc[x, y, k, m] = shard[...]
    for r, shard in ((0, co), (512, lo)):
        wp[x, y, r : r + 128, 0:128] = shard[0:128, :]
        wp[x, y, r : r + 128, 128:256] = shard[128:256, :]
    for m, shard in enumerate((lq, lk, lv)):
        wp[x, y, 128 * (m + 1) : 128 * (m + 2), :] = shard[...]

    barrier = pltpu.get_barrier_semaphore()
    beside = [wrap(c + 1, SIDE * SIDE), wrap(c - 1, SIDE * SIDE)]
    peers = [dev(wrap(x + d, SIDE), y, k, z) for d in (1, 2, 3)]
    peers += [dev(x, wrap(y + d, SIDE), k, z) for d in (1, 2, 3)]
    peers += [partner, up, down, above, below]
    peers += [(chip * 2 + core, z) for chip in beside for core in (0, 1)]
    for peer in peers:
        pl.semaphore_signal(barrier, inc=1, device_id=peer, device_id_type=MESH)
    slot_row = bp_ref[...] - (seq * 128 - 64)

    def slots(first, count):
        shape = (ROWS, count)
        return lax.broadcasted_iota(jnp.int32, shape, 0) == slot_row[:, first : first + count]

    ones = slots(0, bs.shape[0]).astype(F32)
    count = jnp.maximum(jnp.sum(ones, axis=1, keepdims=True), 1.0)
    onehot[...] = ones.astype(BF)
    load.wait()

    @pl.loop(0, 4)
    def _(i):
        cols = pl.ds(pl.multiple_of(i * 256, 256), 256)
        pooled[:, cols] = (dot(onehot[...], bs[:, cols]) / count).astype(BF)

    pl.semaphore_wait(barrier, len(peers))

    phase_start(wc, 0, 1, (1, 2, 3))
    phase_start(wp, 1, 1, (1, 2, 3))

    def hand_over(half, d):
        held = piece(wc, half, 2, -d, *span(0, half))
        send(held, held, es.at[7 + 4 * half + d], er.at[7 + 4 * half + d], partner)

    phase_wait(wc, 0, 1, (1, 2, 3))
    phase_start(wc, 0, 2, (1, 3, 2))
    for half in range(2):
        hand_over(half, 0)
    phase_wait(wp, 1, 1, (1, 2, 3))
    phase_start(wp, 1, 2, (1, 3))
    for d in (1, 3, 2):
        phase_wait(wc, 0, 2, (d,))
        for half in range(2):
            hand_over(half, d)
    relay_start(wp, 1)
    for half in range(2):
        for d in range(SIDE):
            rows = pl.ds(*span(0, half))
            if half == 0:
                theirs = wc.at[:, wrap(y - d, SIDE), 1 - k, :, rows, :]
            else:
                theirs = wc.at[wrap(x - d, SIDE), :, 1 - k, :, rows, :]
            arrive(theirs, es.at[7 + 4 * half + d], er.at[7 + 4 * half + d])

    def cross(m):
        return wc[:, :, :, m].reshape(bs.shape[1], 256)

    phase_start(wp, 2, 1, (1, 3, 2))
    query = dot(pooled[...], cross(0)).astype(BF)
    heads, totals = [0.0, 0.0], [0.0, 0.0]
    for i in range(4):
        part = slice(i * 256, (i + 1) * 256)
        key = dot(bs[part, :], cross(1)).astype(BF)
        value = dot(bs[part, :], cross(2)).astype(BF)
        mask = slots(i * 256, 256)
        for h in range(2):
            cols = slice(h * 128, (h + 1) * 128)
            weight = jnp.where(mask, capped(dot_t(query[:, cols], key[:, cols])), 0.0)
            totals[h] = totals[h] + weight[:, 0:128] + weight[:, 128:256]
            heads[h] = heads[h] + dot(weight.astype(BF), value[:, cols])
    for h in range(2):
        total = jnp.sum(totals[h], axis=1, keepdims=True)
        total = jnp.where(total > 0.0, total, 1.0)
        wbuf[k, :, h * 128 : (h + 1) * 128] = (heads[h] / total).astype(BF)

    send(wbuf.at[k], wbuf.at[k], es.at[1], er.at[1], partner)
    near = wrap(c + 2 * k - 1, SIDE * SIDE)
    edge = wbuf.at[k, pl.ds(pl.multiple_of(k * 192, 64), 64), :]
    for core in (0, 1):
        send(edge, e1b.at[1 - k], es.at[2 + core], er.at[3 - k], (near * 2 + core, z))
    arrive(wbuf.at[1 - k], es.at[1], er.at[1])
    arrive(e1b.at[0], es.at[2], er.at[2])
    arrive(e1b.at[1], es.at[3], er.at[3])
    xbuf[0:64, :] = wbuf[0, 64:128, :] + e1b[0]
    xbuf[64:192, :] = wbuf[0, 128:256, :] + wbuf[1, 0:128, :]
    xbuf[192:256, :] = wbuf[1, 128:192, :] + e1b[1]
    relay_wait(wp, 1)
    phase_wait(wp, 2, 1, (1, 2, 3))
    phase_start(wp, 2, 2, (1, 3))

    def chunk_of(g, j):
        r, n = GROUPS[g]
        return wp[lax.div(j, SIDE), lax.rem(j, SIDE), r : r + n, :]

    def main_slot(side, m):
        return m if side == 0 else 2 * HOPS + m - 1

    def side_slot(side, m):
        return HOPS + m if side == 0 else 3 * HOPS - 1 + m

    def received(w, slot, p):
        rows = slice(p * STRIP, (p + 1) * STRIP)
        arrive(rrecv.at[w, slot, rows], rss.at[w, slot, p], rsr.at[w, slot, p])
        return rrecv[w, slot, rows].astype(F32)

    def give(w, slot, p, value, target):
        rows = slice(p * STRIP, (p + 1) * STRIP)
        rsend[w, slot, rows] = value.astype(BF)
        send(rsend.at[w, slot, rows], rrecv.at[w, slot, rows], rss.at[w, slot, p], rsr.at[w, slot, p], target)

    def reduce_depth(w, part, hook, result):
        def share(side, away):
            return part(wrap(z + away if side == 0 else z - away, DEPTH))

        def strips(term):
            return [term[p * STRIP : (p + 1) * STRIP] for p in range(PARTS)]

        far, near = (above, below), (up, down)

        def give_step(m, p, mains, sides):
            for side, main in mains.items():
                give(w, main_slot(side, m), p, main, far[side])
            for side in range(2):
                give(w, side_slot(side, m), p, sides[side][p], near[side])

        first_main = strips(share(0, 2 * HOPS))
        first_sides = [strips(share(side, 2 * HOPS - 1)) for side in range(2)]
        for p in range(PARTS):
            give_step(0, p, {0: first_main[p]}, first_sides)
        for m in range(HOPS):
            last = m + 1 == HOPS
            away = 2 * (HOPS - 1 - m)
            terms = [strips(share(side, away)) for side in range(1 if last else 2)]
            sides = None if last else [strips(share(side, away - 1)) for side in range(2)]
            for p in range(PARTS):
                sums = [received(w, side_slot(side, m), p) for side in range(2)]
                for side in range(2 if m else 1):
                    sums[side] = sums[side] + received(w, main_slot(side, m), p)
                if last:
                    result(slice(p * STRIP, (p + 1) * STRIP), terms[0][p] + sums[0] + sums[1])
                else:
                    give_step(m + 1, p, {side: terms[side][p] + sums[side] for side in range(2)}, sides)
            hook(m)

    def first_part(j):
        w = chunk_of(1, j)
        return dot(xbuf[:, 0:128], w[:, 0:128]) + dot(xbuf[:, 128:256], w[:, 128:256])

    def first_hook(u):
        if u == 1:
            relay_start(wp, 2)
        if u == 2:
            phase_start(wp, 3, 1, (1, 2, 3))

    def pass_on(m, p):
        part = pl.ds(p * STRIP, STRIP)
        for side, far, near in ((0, above, up), (1, below, down)):
            strip = ag.at[wrap(z - 2 * m if side == 0 else z + 2 * m, DEPTH), part]
            if side == 0 or m + 1 < HOPS:
                slot = main_slot(side, m + side)
                send(strip, strip, ags.at[slot, p], agr.at[slot, p], far)
            slot = side_slot(side, m)
            send(strip, strip, ags.at[slot, p], agr.at[slot, p], near)

    def first_result(rows, value):
        ag[z, rows] = value.astype(BF)
        latent[rows] = ag[z, rows]
        pass_on(0, rows.start // STRIP)

    reduce_depth(0, first_part, first_hook, first_result)

    def project(js, fresh):
        pieces, weights = [], []
        squares = None
        for j in js:
            held = ag[j].astype(F32)
            squares = held * held if squares is None else squares + held * held
            pieces.append((held * gain[pl.ds(2 * j + k, 1), :]).astype(BF))
            weights.append(chunk_of(2, j))
        left = pieces[0] if len(js) == 1 else jnp.concatenate(pieces, axis=1)
        sq[...] = squares if fresh else sq[...] + squares
        for m in range(3):
            rows = [w[m * 128 : (m + 1) * 128, :] for w in weights]
            right = rows[0] if len(js) == 1 else jnp.concatenate(rows, axis=0)
            term = dot(left, right)
            for h in range(2):
                at = (h, slice(None), PLACE[m])
                piece_of = term[:, h * 128 : (h + 1) * 128]
                acc[at] = piece_of if fresh else acc[at] + piece_of

    relay_wait(wp, 2)
    project([z], True)
    def take(j, slot, p):
        arrive(ag.at[j, pl.ds(p * STRIP, STRIP)], ags.at[slot, p], agr.at[slot, p])

    held = None
    for m in range(HOPS):
        mains = [(main_slot(0, m), wrap(z - 2 * (m + 1), DEPTH))]
        if m + 1 < HOPS:
            mains.append((main_slot(1, m + 1), wrap(z + 2 * (m + 1), DEPTH)))
        sides = [(side_slot(0, m), wrap(z - 1 - 2 * m, DEPTH)), (side_slot(1, m), wrap(z + 1 + 2 * m, DEPTH))]
        for p in range(PARTS):
            if m + 1 == HOPS and p == PARTS - 1:
                for slot, j in sides:
                    for strip in range(PARTS):
                        take(j, slot, strip)
                project([j for _, j in sides], False)
            for slot, j in mains:
                take(j, slot, p)
            if m + 1 < HOPS:
                pass_on(m + 1, p)
            if p == 0 and held is not None:
                project(held, False)
        if m + 1 < HOPS:
            for slot, j in sides:
                for p in range(PARTS):
                    take(j, slot, p)
            project([j for _, j in sides], False)
        held = [j for _, j in mains]
        if m == 1:
            phase_wait(wp, 3, 1, (1, 2, 3))
            phase_start(wp, 3, 2, (1, 3))
    project(held, False)

    acc[1 - k, :, PLACE[3]] = sq[...]
    first, last = (slice(None), pl.ds(0, 384)), (slice(None), pl.ds(384, 128))
    send(acc.at[(1 - k,) + first], e2.at[first], es.at[4], er.at[4], partner)
    send(acc.at[(1 - k,) + last], e2.at[last], es.at[0], er.at[0], partner)
    arrive(e2.at[first], es.at[4], er.at[4])
    mean = jnp.sum(sq[...] + e2[:, PLACE[3]], axis=1, keepdims=True) / (2 * DEPTH * 128)
    factor = lax.rsqrt(mean + EPS)

    def joined(m):
        return ((acc[k, :, PLACE[m]] + e2[:, PLACE[m]]) * factor).astype(BF)

    kvb[x, y, :, 0:128] = joined(1)
    kvb[x, y, :, 128:256] = joined(2)

    def kv_piece(half, q, d, r, n):
        px, py = (wrap(x - q, SIDE), wrap(y - d, SIDE)) if half == 0 else (wrap(x - d, SIDE), wrap(y - q, SIDE))
        return kvb.at[px, py, pl.ds(r, n), :]

    def kv_on(q):
        for half in range(2):
            held = kv_piece(half, q, 0, *span(4, half))
            for side, d in ((0, 1), (1, 3)):
                send(held, held, kvs.at[half, side, q], kvr.at[half, side, q], along(half, 2, d))

    def kv_relay(q):
        for half in range(2):
            r, n = span(4, half)
            for side, d in ((0, 1), (1, 3)):
                arrive(kv_piece(half, q, d, r, n), kvs.at[half, side, q], kvr.at[half, side, q])
                part = kv_piece(half, q, d, r + side * (n // 2), n // 2)
                send(part, part, kvs.at[half, 2 + side, q], kvr.at[half, 2 + side, q], along(half, 2, d))

    def kv_last(q):
        for half in range(2):
            r, n = span(4, half)
            for side in range(2):
                part = kv_piece(half, q, 2, r + side * (n // 2), n // 2)
                arrive(part, kvs.at[half, 2 + side, q], kvr.at[half, 2 + side, q])

    phase_start(kvb, 4, 1, (1, 3, 2))
    kv_on(0)
    arrive(e2.at[last], es.at[0], er.at[0])
    qs[...] = joined(0)

    def attend(blocks):
        value = total = None
        for dx, dy in blocks:
            px, py = wrap(x + dx, SIDE), wrap(y + dy, SIDE)
            weight = capped(dot_t(qs[...], kvb[px, py, :, 0:128]))
            if (dx, dy) == (0, 0):
                shape = (ROWS, ROWS)
                seen = lax.broadcasted_iota(jnp.int32, shape, 1) <= lax.broadcasted_iota(jnp.int32, shape, 0)
                weight = jnp.where(seen, weight, 0.0)
            else:
                weight = weight * jnp.where(px * SIDE + py < c, 1.0, 0.0)
            term = dot(weight.astype(BF), kvb[px, py, :, 128:256])
            mass = weight[:, 0:128] + weight[:, 128:256]
            value = term if value is None else value + term
            total = mass if total is None else total + mass
        own = blocks[0] == (0, 0)
        oacc[...] = value if own else oacc[...] + value
        lacc[...] = total if own else lacc[...] + total

    attend([(0, 0)])
    for d in (1, 3):
        phase_wait(kvb, 4, 1, (d,))
        kv_on(d)
    kv_relay(0)
    phase_wait(kvb, 4, 1, (2,))
    kv_on(2)
    attend([(1, 0), (3, 0), (0, 1), (0, 3)])
    kv_relay(1)
    kv_relay(3)
    attend([(1, 1), (1, 3), (3, 1), (3, 3)])
    kv_relay(2)
    relay_start(wp, 3)
    kv_last(0)
    attend([(2, 0), (0, 2)])
    kv_last(1)
    kv_last(3)
    attend([(2, 1), (2, 3), (1, 2), (3, 2)])
    kv_last(2)
    attend([(2, 2)])
    relay_wait(wp, 3)

    total = jnp.sum(lacc[...], axis=1, keepdims=True)
    att[k] = (oacc[...] / total).astype(BF)
    send(att.at[k], att.at[k], es.at[5], er.at[5], partner)
    arrive(att.at[1 - k], es.at[5], er.at[5])

    def second_part(j):
        w = chunk_of(3, j)
        return dot(att[0], w[:, 0:128]) + dot(att[1], w[:, 128:256])

    def second_result(rows, value):
        fin_s[rows] = (latent[rows].astype(F32) + value).astype(BF)

    reduce_depth(1, second_part, lambda m: None, second_result)
    theirs = fin_s.at[pl.ds(pl.multiple_of((1 - k) * 128, 128), 128), :]
    send(theirs, fin_r, es.at[6], er.at[6], partner)
    mine = pl.ds(pl.multiple_of(k * 128, 128), 128)
    out_ref[:, mine] = fin_s[mine, :]
    arrive(fin_r, es.at[6], er.at[6])
    out_ref[:, pl.ds(pl.multiple_of((1 - k) * 128, 128), 128)] = fin_r[...]
    for copy in started:
        copy.wait_send()


def per_device(
    byte_states, byte_patch, patch_len, cross_query, cross_key, cross_value, cross_out, norm_gain,
    latent_query, latent_key, latent_value, latent_out,
):
    vmem = pl.BlockSpec(memory_space=pltpu.VMEM)
    bytes_here, width = byte_states.shape
    dma = pltpu.SemaphoreType.DMA
    groups = len(GROUPS)
    block = (ROWS, HEAD_DIM)
    return pl.pallas_call(
        kernel,
        out_shape=jax.ShapeDtypeStruct((128, 256), BF),
        in_specs=[pl.BlockSpec(memory_space=pl.ANY)] + [vmem] * 10,
        out_specs=vmem,
        scratch_shapes=[
            pltpu.VMEM((bytes_here, width), BF),
            pltpu.VMEM((SIDE, SIDE, PACKED, 256), BF),
            pltpu.VMEM((SIDE, SIDE, 2, 3, 32, 256), BF),
            pltpu.VMEM((ROWS, width), BF),
            pltpu.VMEM((ROWS, bytes_here), BF),
            pltpu.VMEM((2, ROWS, 256), BF),
            pltpu.VMEM((2, 64, 256), BF),
            pltpu.VMEM((ROWS, 256), BF),
            pltpu.VMEM((2, DEPTH - 1) + block, BF),
            pltpu.VMEM((2, DEPTH - 1) + block, BF),
            pltpu.VMEM((DEPTH,) + block, BF),
            pltpu.VMEM((2, ROWS, 512), F32),
            pltpu.VMEM(block, F32),
            pltpu.VMEM((ROWS, 512), F32),
            pltpu.VMEM(block, BF),
            pltpu.VMEM((SIDE, SIDE, ROWS, 256), BF),
            pltpu.VMEM(block, F32),
            pltpu.VMEM(block, F32),
            pltpu.VMEM((2,) + block, BF),
            pltpu.VMEM(block, BF),
            pltpu.VMEM(block, BF),
            pltpu.VMEM((128, HEAD_DIM), BF),
            dma,
            dma((groups, 2, 3)),
            dma((groups, 2, 3)),
            dma((groups, 2, 3)),
            dma((groups, 2, 3)),
            dma((groups, 2, 2)),
            dma((groups, 2, 2)),
            dma((2, DEPTH - 1, PARTS)),
            dma((2, DEPTH - 1, PARTS)),
            dma((DEPTH - 1, PARTS)),
            dma((DEPTH - 1, PARTS)),
            dma((15,)),
            dma((15,)),
            dma((2, SIDE, SIDE)),
            dma((2, SIDE, SIDE)),
        ],
        compiler_params=pltpu.CompilerParams(
            collective_id=0, has_side_effects=True, vmem_limit_bytes=60 * 1024 * 1024
        ),
        name="patches",
    )(
        byte_states, byte_patch.reshape(1, -1), cross_query, cross_key, cross_value, cross_out,
        norm_gain.reshape(-1, HEAD_DIM), latent_query, latent_key, latent_value, latent_out,
    )


def solution(mesh):
    return jax.shard_map(
        per_device,
        mesh=mesh,
        in_specs=(
            P("seq", None), P("seq"), P(), P("seq", "tensor"), P("seq", "tensor"), P("seq", "tensor"),
            P("tensor", "seq"), P(), P("seq", "tensor"), P("seq", "tensor"), P("seq", "tensor"), P("tensor", "seq"),
        ),
        out_specs=P("seq", "tensor"),
        check_vma=False,
    )
```

```python
import math

import jax
import jax.numpy as jnp
from jax import lax
from jax.experimental import pallas as pl
from jax.experimental.pallas import tpu as pltpu
from jax.sharding import PartitionSpec as P

MESH = pl.DeviceIdType.MESH
HEAD_DIM = 128
SIDE = 4
DEPTH = 16
ROWS = 256
CAP = 30.0
EPS = 1e-05
TEMPER = 1.0 / (CAP * math.sqrt(HEAD_DIM))
BF = jnp.bfloat16
F32 = jnp.float32

GROUPS = ((0, 32), (0, 128), (128, 384), (512, 128), (0, ROWS))
PACKED = 640
HOPS = DEPTH // 4
PARTS = 4
STRIP = ROWS // PARTS
ORDER = (1, 2, 0, 3)
PLACE = (slice(384, 512), slice(0, 128), slice(128, 256), slice(256, 384))


def dot(a, b):
    return jnp.dot(a, b, preferred_element_type=F32)


def dot_t(a, b):
    return lax.dot_general(a, b, (((1,), (1,)), ((), ())), preferred_element_type=F32)


def capped(raw):
    return jnp.exp(CAP * jnp.tanh(raw * TEMPER))


def kernel(
    bs_in, bp_in, cq, ck, cv, co, gain_in, lq, lk, lv, lo,
    out_ref,
    bs, bp_ref, gain, wp, wc, pooled, onehot, wbuf, e1b, xbuf, rsend, rrecv, ag, acc, sq, e2, qs, kvb, oacc, lacc, att, latent, fin_s, fin_r,
    bs_sem, p1s, p1r, p2s, p2r, rls, rlr, rss, rsr, ags, agr, es, er, kvs, kvr,
):
    seq, z = lax.axis_index("seq"), lax.axis_index("tensor")
    k, c = lax.rem(seq, 2), lax.div(seq, 2)
    x, y = lax.div(c, SIDE), lax.rem(c, SIDE)
    started = []

    def wrap(i, n):
        return lax.rem(i + n, n)

    def dev(px, py, core, depth):
        return ((px * SIDE + py) * 2 + core, depth)

    def remote(src, dst, ssem, rsem, target):
        return pltpu.make_async_remote_copy(
            src_ref=src, dst_ref=dst, send_sem=ssem, recv_sem=rsem, device_id=target, device_id_type=MESH
        )

    def send(src, dst, ssem, rsem, target):
        copy = remote(src, dst, ssem, rsem, target)
        copy.start()
        started.append(copy)

    def arrive(dst, ssem, rsem):
        remote(dst, dst, ssem, rsem, partner).wait_recv()

    partner = (seq + 1 - 2 * k, z)
    up, down = (seq, wrap(z + 1, DEPTH)), (seq, wrap(z - 1, DEPTH))
    above, below = (seq, wrap(z + 2, DEPTH)), (seq, wrap(z - 2, DEPTH))

    def along(half, phase, d):
        if (half == 0) == (phase == 1):
            return dev(wrap(x + d, SIDE), y, k, z)
        return dev(x, wrap(y + d, SIDE), k, z)

    def piece(buf, half, phase, d, r, n):
        part = pl.ds(r, n)
        if buf is wc:
            if half == 0:
                across = wrap(x + d, SIDE) if phase == 1 else slice(None)
                return wc.at[across, y if phase == 1 else wrap(y + d, SIDE), k, :, part, :]
            across = slice(None) if phase == 2 else wrap(y + d, SIDE)
            return wc.at[x if phase == 1 else wrap(x + d, SIDE), across, k, :, part, :]
        if half == 0:
            return buf.at[wrap(x + d, SIDE), y, part, :] if phase == 1 else buf.at[:, wrap(y + d, SIDE), part, :]
        return buf.at[x, wrap(y + d, SIDE), part, :] if phase == 1 else buf.at[wrap(x + d, SIDE), :, part, :]

    def span(g, half):
        r, n = GROUPS[g]
        return r + half * (n // 2), n // 2

    def phase_start(buf, g, phase, steps):
        ssem, rsem = (p1s, p1r) if phase == 1 else (p2s, p2r)
        for half in range(2):
            own = piece(buf, half, phase, 0, *span(g, half))
            for d in steps:
                send(own, own, ssem.at[g, half, d - 1], rsem.at[g, half, d - 1], along(half, phase, d))

    def phase_wait(buf, g, phase, steps):
        ssem, rsem = (p1s, p1r) if phase == 1 else (p2s, p2r)
        for half in range(2):
            for d in steps:
                arrive(piece(buf, half, phase, -d, *span(g, half)), ssem.at[g, half, d - 1], rsem.at[g, half, d - 1])

    def relay_start(buf, g):
        for half in range(2):
            r, n = span(g, half)
            for side, d in ((0, 1), (1, 3)):
                arrive(piece(buf, half, 2, -d, r, n), p2s.at[g, half, d - 1], p2r.at[g, half, d - 1])
                part = piece(buf, half, 2, -d, r + side * (n // 2), n // 2)
                send(part, part, rls.at[g, half, side], rlr.at[g, half, side], along(half, 2, d))

    def relay_wait(buf, g):
        for half in range(2):
            r, n = span(g, half)
            for side in range(2):
                arrive(piece(buf, half, 2, 2, r + side * (n // 2), n // 2), rls.at[g, half, side], rlr.at[g, half, side])

    low, high = pl.ds(0, 128), pl.ds(128, 128)
    moves = [(bp_in, bp_ref), (bs_in, bs), (gain_in, gain)]
    moves += [(shard, wc.at[x, y, k, m]) for m, shard in enumerate((cq, ck, cv))]
    for r, shard in ((0, co), (512, lo)):
        moves += [(shard.at[half, :], wp.at[x, y, pl.ds(r, 128), half]) for half in (low, high)]
    moves += [(shard, wp.at[x, y, pl.ds(128 * (m + 1), 128), :]) for m, shard in enumerate((lq, lk, lv))]
    loads = [pltpu.make_async_copy(src, dst, bs_sem.at[n]) for n, (src, dst) in enumerate(moves)]
    for copy in loads:
        copy.start()

    barrier = pltpu.get_barrier_semaphore()
    beside = [wrap(c + 1, SIDE * SIDE), wrap(c - 1, SIDE * SIDE)]
    peers = [dev(wrap(x + d, SIDE), y, k, z) for d in (1, 2, 3)]
    peers += [dev(x, wrap(y + d, SIDE), k, z) for d in (1, 2, 3)]
    peers += [partner, up, down, above, below]
    peers += [(chip * 2 + core, z) for chip in beside for core in (0, 1)]
    for peer in peers:
        pl.semaphore_signal(barrier, inc=1, device_id=peer, device_id_type=MESH)
    loads[0].wait()
    slot_row = bp_ref[...] - (seq * 128 - 64)

    def slots(first, count):
        shape = (ROWS, count)
        return lax.broadcasted_iota(jnp.int32, shape, 0) == slot_row[:, first : first + count]

    ones = slots(0, bs.shape[0]).astype(F32)
    count = jnp.maximum(jnp.sum(ones, axis=1, keepdims=True), 1.0)
    onehot[...] = ones.astype(BF)
    loads[1].wait()

    @pl.loop(0, 4)
    def _(i):
        cols = pl.ds(pl.multiple_of(i * 256, 256), 256)
        pooled[:, cols] = (dot(onehot[...], bs[:, cols]) / count).astype(BF)

    for copy in loads[2:]:
        copy.wait()
    pl.semaphore_wait(barrier, len(peers))

    phase_start(wc, 0, 1, (1, 2, 3))
    phase_start(wp, 1, 1, (1, 2, 3))

    def hand_over(half, d):
        held = piece(wc, half, 2, -d, *span(0, half))
        send(held, held, es.at[7 + 4 * half + d], er.at[7 + 4 * half + d], partner)

    phase_wait(wc, 0, 1, (1, 2, 3))
    phase_start(wc, 0, 2, (1, 3, 2))
    for half in range(2):
        hand_over(half, 0)
    phase_wait(wp, 1, 1, (1, 2, 3))
    phase_start(wp, 1, 2, (1, 3))
    for d in (1, 3, 2):
        phase_wait(wc, 0, 2, (d,))
        for half in range(2):
            hand_over(half, d)
    relay_start(wp, 1)
    for half in range(2):
        for d in range(SIDE):
            rows = pl.ds(*span(0, half))
            if half == 0:
                theirs = wc.at[:, wrap(y - d, SIDE), 1 - k, :, rows, :]
            else:
                theirs = wc.at[wrap(x - d, SIDE), :, 1 - k, :, rows, :]
            arrive(theirs, es.at[7 + 4 * half + d], er.at[7 + 4 * half + d])

    def cross(m):
        return wc[:, :, :, m].reshape(bs.shape[1], 256)

    phase_start(wp, 2, 1, (1, 3, 2))
    query = dot(pooled[...], cross(0)).astype(BF)
    heads, totals = [0.0, 0.0], [0.0, 0.0]
    for i in range(4):
        part = slice(i * 256, (i + 1) * 256)
        key = dot(bs[part, :], cross(1)).astype(BF)
        value = dot(bs[part, :], cross(2)).astype(BF)
        mask = slots(i * 256, 256)
        for h in range(2):
            cols = slice(h * 128, (h + 1) * 128)
            weight = jnp.where(mask, capped(dot_t(query[:, cols], key[:, cols])), 0.0)
            totals[h] = totals[h] + weight[:, 0:128] + weight[:, 128:256]
            heads[h] = heads[h] + dot(weight.astype(BF), value[:, cols])
    for h in range(2):
        total = jnp.sum(totals[h], axis=1, keepdims=True)
        total = jnp.where(total > 0.0, total, 1.0)
        wbuf[k, :, h * 128 : (h + 1) * 128] = (heads[h] / total).astype(BF)

    send(wbuf.at[k], wbuf.at[k], es.at[1], er.at[1], partner)
    near = wrap(c + 2 * k - 1, SIDE * SIDE)
    edge = wbuf.at[k, pl.ds(pl.multiple_of(k * 192, 64), 64), :]
    for core in (0, 1):
        send(edge, e1b.at[1 - k], es.at[2 + core], er.at[3 - k], (near * 2 + core, z))
    arrive(wbuf.at[1 - k], es.at[1], er.at[1])
    xbuf[64:192, :] = wbuf[0, 128:256, :] + wbuf[1, 0:128, :]
    relay_wait(wp, 1)

    def first_late():
        arrive(e1b.at[0], es.at[2], er.at[2])
        arrive(e1b.at[1], es.at[3], er.at[3])
        xbuf[0:64, :] = wbuf[0, 64:128, :] + e1b[0]
        xbuf[192:256, :] = wbuf[1, 128:192, :] + e1b[1]
        phase_wait(wp, 2, 1, (1, 2, 3))
        phase_start(wp, 2, 2, (1, 3))

    def chunk_of(g, j):
        r, n = GROUPS[g]
        return wp[lax.div(j, SIDE), lax.rem(j, SIDE), r : r + n, :]

    def main_slot(side, m):
        return m if side == 0 else 2 * HOPS + m - 1

    def side_slot(side, m):
        return HOPS + m if side == 0 else 3 * HOPS - 1 + m

    def received(w, slot, p):
        rows = slice(p * STRIP, (p + 1) * STRIP)
        arrive(rrecv.at[w, slot, rows], rss.at[w, slot, p], rsr.at[w, slot, p])
        return rrecv[w, slot, rows].astype(F32)

    def give(w, slot, p, value, target):
        rows = slice(p * STRIP, (p + 1) * STRIP)
        rsend[w, slot, rows] = value.astype(BF)
        send(rsend.at[w, slot, rows], rrecv.at[w, slot, rows], rss.at[w, slot, p], rsr.at[w, slot, p], target)

    def reduce_depth(w, part, late, hook, result):
        def share(side, away, rows=slice(0, ROWS)):
            return part(wrap(z + away if side == 0 else z - away, DEPTH), rows)

        def strips(term):
            return [term[p * STRIP : (p + 1) * STRIP] for p in range(PARTS)]

        far, near = (above, below), (up, down)

        def give_step(m, p, mains, sides):
            for side, main in mains.items():
                give(w, main_slot(side, m), p, main, far[side])
            for side in range(2):
                give(w, side_slot(side, m), p, sides[side], near[side])

        for p in ORDER:
            if p == ORDER[2]:
                late()
            rows = slice(p * STRIP, (p + 1) * STRIP)
            give_step(0, p, {0: share(0, 2 * HOPS, rows)}, [share(side, 2 * HOPS - 1, rows) for side in range(2)])
        for m in range(HOPS):
            last = m + 1 == HOPS
            away = 2 * (HOPS - 1 - m)
            terms = [strips(share(side, away)) for side in range(1 if last else 2)]
            sides = None if last else [strips(share(side, away - 1)) for side in range(2)]
            for p in ORDER:
                sums = [received(w, side_slot(side, m), p) for side in range(2)]
                for side in range(2 if m else 1):
                    sums[side] = sums[side] + received(w, main_slot(side, m), p)
                if last:
                    result(slice(p * STRIP, (p + 1) * STRIP), terms[0][p] + sums[0] + sums[1])
                else:
                    give_step(m + 1, p, {side: terms[side][p] + sums[side] for side in range(2)}, [sides[0][p], sides[1][p]])
            hook(m)

    def first_part(j, rows):
        w = chunk_of(1, j)
        return dot(xbuf[rows, 0:128], w[:, 0:128]) + dot(xbuf[rows, 128:256], w[:, 128:256])

    def first_hook(u):
        if u == 1:
            relay_start(wp, 2)
        if u == 2:
            phase_start(wp, 3, 1, (1, 2, 3))

    def pass_on(m, p):
        part = pl.ds(p * STRIP, STRIP)
        for side, far, near in ((0, above, up), (1, below, down)):
            strip = ag.at[wrap(z - 2 * m if side == 0 else z + 2 * m, DEPTH), part]
            if side == 0 or m + 1 < HOPS:
                slot = main_slot(side, m + side)
                send(strip, strip, ags.at[slot, p], agr.at[slot, p], far)
            slot = side_slot(side, m)
            send(strip, strip, ags.at[slot, p], agr.at[slot, p], near)

    def first_result(rows, value):
        ag[z, rows] = value.astype(BF)
        latent[rows] = ag[z, rows]
        pass_on(0, rows.start // STRIP)

    reduce_depth(0, first_part, first_late, first_hook, first_result)

    def project(js, fresh):
        pieces, weights = [], []
        squares = None
        for j in js:
            held = ag[j].astype(F32)
            squares = held * held if squares is None else squares + held * held
            pieces.append((held * gain[pl.ds(2 * j + k, 1), :]).astype(BF))
            weights.append(chunk_of(2, j))
        left = pieces[0] if len(js) == 1 else jnp.concatenate(pieces, axis=1)
        sq[...] = squares if fresh else sq[...] + squares
        for m in range(3):
            rows = [w[m * 128 : (m + 1) * 128, :] for w in weights]
            right = rows[0] if len(js) == 1 else jnp.concatenate(rows, axis=0)
            term = dot(left, right)
            for h in range(2):
                at = (h, slice(None), PLACE[m])
                piece_of = term[:, h * 128 : (h + 1) * 128]
                acc[at] = piece_of if fresh else acc[at] + piece_of

    relay_wait(wp, 2)
    project([z], True)
    def take(j, slot, p):
        arrive(ag.at[j, pl.ds(p * STRIP, STRIP)], ags.at[slot, p], agr.at[slot, p])

    held = None
    for m in range(HOPS):
        mains = [(main_slot(0, m), wrap(z - 2 * (m + 1), DEPTH))]
        if m + 1 < HOPS:
            mains.append((main_slot(1, m + 1), wrap(z + 2 * (m + 1), DEPTH)))
        sides = [(side_slot(0, m), wrap(z - 1 - 2 * m, DEPTH)), (side_slot(1, m), wrap(z + 1 + 2 * m, DEPTH))]
        for p in ORDER:
            if m + 1 == HOPS and p == ORDER[-1]:
                for slot, j in sides:
                    for strip in range(PARTS):
                        take(j, slot, strip)
                project([j for _, j in sides], False)
            for slot, j in mains:
                take(j, slot, p)
            if m + 1 < HOPS:
                pass_on(m + 1, p)
            if p == ORDER[0] and held is not None:
                project(held, False)
        if m + 1 < HOPS:
            for slot, j in sides:
                for p in range(PARTS):
                    take(j, slot, p)
            project([j for _, j in sides], False)
        held = [j for _, j in mains]
        if m == 1:
            phase_wait(wp, 3, 1, (1, 2, 3))
            phase_start(wp, 3, 2, (1, 3))
    project(held, False)

    acc[1 - k, :, PLACE[3]] = sq[...]
    first, last = (slice(None), pl.ds(0, 384)), (slice(None), pl.ds(384, 128))
    send(acc.at[(1 - k,) + first], e2.at[first], es.at[4], er.at[4], partner)
    send(acc.at[(1 - k,) + last], e2.at[last], es.at[0], er.at[0], partner)
    arrive(e2.at[first], es.at[4], er.at[4])
    mean = jnp.sum(sq[...] + e2[:, PLACE[3]], axis=1, keepdims=True) / (2 * DEPTH * 128)
    factor = lax.rsqrt(mean + EPS)

    def joined(m):
        return ((acc[k, :, PLACE[m]] + e2[:, PLACE[m]]) * factor).astype(BF)

    kvb[x, y, :, 0:128] = joined(1)
    kvb[x, y, :, 128:256] = joined(2)

    def kv_piece(half, q, d, r, n):
        px, py = (wrap(x - q, SIDE), wrap(y - d, SIDE)) if half == 0 else (wrap(x - d, SIDE), wrap(y - q, SIDE))
        return kvb.at[px, py, pl.ds(r, n), :]

    def kv_on(q):
        for half in range(2):
            held = kv_piece(half, q, 0, *span(4, half))
            for side, d in ((0, 1), (1, 3)):
                send(held, held, kvs.at[half, side, q], kvr.at[half, side, q], along(half, 2, d))

    def kv_relay(q):
        for half in range(2):
            r, n = span(4, half)
            for side, d in ((0, 1), (1, 3)):
                arrive(kv_piece(half, q, d, r, n), kvs.at[half, side, q], kvr.at[half, side, q])
                part = kv_piece(half, q, d, r + side * (n // 2), n // 2)
                send(part, part, kvs.at[half, 2 + side, q], kvr.at[half, 2 + side, q], along(half, 2, d))

    def kv_last(q):
        for half in range(2):
            r, n = span(4, half)
            for side in range(2):
                part = kv_piece(half, q, 2, r + side * (n // 2), n // 2)
                arrive(part, kvs.at[half, 2 + side, q], kvr.at[half, 2 + side, q])

    phase_start(kvb, 4, 1, (1, 3, 2))
    kv_on(0)
    arrive(e2.at[last], es.at[0], er.at[0])
    qs[...] = joined(0)

    def attend(blocks):
        value = total = None
        for dx, dy in blocks:
            px, py = wrap(x + dx, SIDE), wrap(y + dy, SIDE)
            weight = capped(dot_t(qs[...], kvb[px, py, :, 0:128]))
            if (dx, dy) == (0, 0):
                shape = (ROWS, ROWS)
                seen = lax.broadcasted_iota(jnp.int32, shape, 1) <= lax.broadcasted_iota(jnp.int32, shape, 0)
                weight = jnp.where(seen, weight, 0.0)
            else:
                weight = weight * jnp.where(px * SIDE + py < c, 1.0, 0.0)
            term = dot(weight.astype(BF), kvb[px, py, :, 128:256])
            mass = weight[:, 0:128] + weight[:, 128:256]
            value = term if value is None else value + term
            total = mass if total is None else total + mass
        own = blocks[0] == (0, 0)
        oacc[...] = value if own else oacc[...] + value
        lacc[...] = total if own else lacc[...] + total

    attend([(0, 0)])
    for d in (1, 3):
        phase_wait(kvb, 4, 1, (d,))
        kv_on(d)
    kv_relay(0)
    phase_wait(kvb, 4, 1, (2,))
    kv_on(2)
    attend([(1, 0), (3, 0), (0, 1), (0, 3)])
    kv_relay(1)
    kv_relay(3)
    attend([(1, 1), (1, 3), (3, 1), (3, 3)])
    kv_relay(2)
    relay_start(wp, 3)
    kv_last(0)
    attend([(2, 0), (0, 2)])
    kv_last(1)
    kv_last(3)
    attend([(2, 1), (2, 3), (1, 2), (3, 2)])
    kv_last(2)
    attend([(2, 2)])
    relay_wait(wp, 3)

    total = jnp.sum(lacc[...], axis=1, keepdims=True)
    att[k] = (oacc[...] / total).astype(BF)
    send(att.at[k], att.at[k], es.at[5], er.at[5], partner)
    arrive(att.at[1 - k], es.at[5], er.at[5])

    def second_part(j, rows):
        w = chunk_of(3, j)
        return dot(att[0, rows], w[:, 0:128]) + dot(att[1, rows], w[:, 128:256])

    def second_result(rows, value):
        fin_s[rows] = (latent[rows].astype(F32) + value).astype(BF)

    reduce_depth(1, second_part, lambda: None, lambda m: None, second_result)
    theirs = fin_s.at[pl.ds(pl.multiple_of((1 - k) * 128, 128), 128), :]
    send(theirs, fin_r, es.at[6], er.at[6], partner)
    mine = pl.ds(pl.multiple_of(k * 128, 128), 128)
    out_ref[:, mine] = fin_s[mine, :]
    arrive(fin_r, es.at[6], er.at[6])
    out_ref[:, pl.ds(pl.multiple_of((1 - k) * 128, 128), 128)] = fin_r[...]
    for copy in started:
        copy.wait_send()


def per_device(
    byte_states, byte_patch, patch_len, cross_query, cross_key, cross_value, cross_out, norm_gain,
    latent_query, latent_key, latent_value, latent_out,
):
    vmem = pl.BlockSpec(memory_space=pltpu.VMEM)
    bytes_here, width = byte_states.shape
    dma = pltpu.SemaphoreType.DMA
    groups = len(GROUPS)
    block = (ROWS, HEAD_DIM)
    return pl.pallas_call(
        kernel,
        out_shape=jax.ShapeDtypeStruct((128, 256), BF),
        in_specs=[pl.BlockSpec(memory_space=pl.ANY)] * 11,
        out_specs=vmem,
        scratch_shapes=[
            pltpu.VMEM((bytes_here, width), BF),
            pltpu.VMEM((1, bytes_here), jnp.int32),
            pltpu.VMEM((2 * DEPTH, HEAD_DIM), F32),
            pltpu.VMEM((SIDE, SIDE, PACKED, 256), BF),
            pltpu.VMEM((SIDE, SIDE, 2, 3, 32, 256), BF),
            pltpu.VMEM((ROWS, width), BF),
            pltpu.VMEM((ROWS, bytes_here), BF),
            pltpu.VMEM((2, ROWS, 256), BF),
            pltpu.VMEM((2, 64, 256), BF),
            pltpu.VMEM((ROWS, 256), BF),
            pltpu.VMEM((2, DEPTH - 1) + block, BF),
            pltpu.VMEM((2, DEPTH - 1) + block, BF),
            pltpu.VMEM((DEPTH,) + block, BF),
            pltpu.VMEM((2, ROWS, 512), F32),
            pltpu.VMEM(block, F32),
            pltpu.VMEM((ROWS, 512), F32),
            pltpu.VMEM(block, BF),
            pltpu.VMEM((SIDE, SIDE, ROWS, 256), BF),
            pltpu.VMEM(block, F32),
            pltpu.VMEM(block, F32),
            pltpu.VMEM((2,) + block, BF),
            pltpu.VMEM(block, BF),
            pltpu.VMEM(block, BF),
            pltpu.VMEM((128, HEAD_DIM), BF),
            dma((13,)),
            dma((groups, 2, 3)),
            dma((groups, 2, 3)),
            dma((groups, 2, 3)),
            dma((groups, 2, 3)),
            dma((groups, 2, 2)),
            dma((groups, 2, 2)),
            dma((2, DEPTH - 1, PARTS)),
            dma((2, DEPTH - 1, PARTS)),
            dma((DEPTH - 1, PARTS)),
            dma((DEPTH - 1, PARTS)),
            dma((15,)),
            dma((15,)),
            dma((2, SIDE, SIDE)),
            dma((2, SIDE, SIDE)),
        ],
        compiler_params=pltpu.CompilerParams(
            collective_id=0, has_side_effects=True, vmem_limit_bytes=60 * 1024 * 1024
        ),
        name="patches",
    )(
        byte_states, byte_patch.reshape(1, -1), cross_query, cross_key, cross_value, cross_out,
        norm_gain.reshape(-1, HEAD_DIM), latent_query, latent_key, latent_value, latent_out,
    )


def solution(mesh):
    return jax.shard_map(
        per_device,
        mesh=mesh,
        in_specs=(
            P("seq", None), P("seq"), P(), P("seq", "tensor"), P("seq", "tensor"), P("seq", "tensor"),
            P("tensor", "seq"), P(), P("seq", "tensor"), P("seq", "tensor"), P("seq", "tensor"), P("tensor", "seq"),
        ),
        out_specs=P("seq", "tensor"),
        check_vma=False,
    )
```

```python
import math

import jax
import jax.numpy as jnp
from jax import lax
from jax.experimental import pallas as pl
from jax.experimental.pallas import tpu as pltpu
from jax.sharding import PartitionSpec as P

MESH = pl.DeviceIdType.MESH
HEAD_DIM = 128
SIDE = 4
DEPTH = 16
ROWS = 256
CAP = 30.0
EPS = 1e-05
TEMPER = 1.0 / (CAP * math.sqrt(HEAD_DIM))
BF = jnp.bfloat16
F32 = jnp.float32

GROUPS = ((0, 32), (0, 128), (128, 384), (512, 128), (0, ROWS))
PACKED = 640
HOPS = DEPTH // 4
PARTS = 4
STRIP = ROWS // PARTS
ORDER = (1, 2, 0, 3)
PLACE = (slice(384, 512), slice(0, 128), slice(128, 256), slice(256, 384))


def dot(a, b):
    return jnp.dot(a, b, preferred_element_type=F32)


def dot_t(a, b):
    return lax.dot_general(a, b, (((1,), (1,)), ((), ())), preferred_element_type=F32)


def capped(raw):
    return jnp.exp(CAP * jnp.tanh(raw * TEMPER))


def kernel(
    bs_in, bp_in, cq, ck, cv, co, gain_in, lq, lk, lv, lo,
    out_ref,
    bs, bp_ref, gain, wp, wc, pooled, onehot, wbuf, e1b, xbuf, rsend, rrecv, ag, acc, sq, e2, qs, kvb, oacc, lacc, att, latent, fin_s, fin_r,
    bs_sem, p1s, p1r, p2s, p2r, rls, rlr, rss, rsr, ags, agr, es, er, kvs, kvr, wcs, wcr,
):
    seq, z = lax.axis_index("seq"), lax.axis_index("tensor")
    k, c = lax.rem(seq, 2), lax.div(seq, 2)
    x, y = lax.div(c, SIDE), lax.rem(c, SIDE)
    started = []

    def wrap(i, n):
        return lax.rem(i + n, n)

    def dev(px, py, core, depth):
        return ((px * SIDE + py) * 2 + core, depth)

    def remote(src, dst, ssem, rsem, target):
        return pltpu.make_async_remote_copy(
            src_ref=src, dst_ref=dst, send_sem=ssem, recv_sem=rsem, device_id=target, device_id_type=MESH
        )

    def send(src, dst, ssem, rsem, target):
        copy = remote(src, dst, ssem, rsem, target)
        copy.start()
        started.append(copy)

    def arrive(dst, ssem, rsem):
        remote(dst, dst, ssem, rsem, partner).wait_recv()

    partner = (seq + 1 - 2 * k, z)
    up, down = (seq, wrap(z + 1, DEPTH)), (seq, wrap(z - 1, DEPTH))
    above, below = (seq, wrap(z + 2, DEPTH)), (seq, wrap(z - 2, DEPTH))

    def along(half, phase, d):
        if (half == 0) == (phase == 1):
            return dev(wrap(x + d, SIDE), y, k, z)
        return dev(x, wrap(y + d, SIDE), k, z)

    def piece(buf, half, phase, d, r, n):
        part = pl.ds(r, n)
        if buf is wc:
            if half == 0:
                across = wrap(x + d, SIDE) if phase == 1 else slice(None)
                return wc.at[across, y if phase == 1 else wrap(y + d, SIDE), k, :, part, :]
            across = slice(None) if phase == 2 else wrap(y + d, SIDE)
            return wc.at[x if phase == 1 else wrap(x + d, SIDE), across, k, :, part, :]
        if half == 0:
            return buf.at[wrap(x + d, SIDE), y, part, :] if phase == 1 else buf.at[:, wrap(y + d, SIDE), part, :]
        return buf.at[x, wrap(y + d, SIDE), part, :] if phase == 1 else buf.at[wrap(x + d, SIDE), :, part, :]

    def span(g, half):
        r, n = GROUPS[g]
        return r + half * (n // 2), n // 2

    def phase_start(buf, g, phase, steps):
        ssem, rsem = (p1s, p1r) if phase == 1 else (p2s, p2r)
        for half in range(2):
            own = piece(buf, half, phase, 0, *span(g, half))
            for d in steps:
                send(own, own, ssem.at[g, half, d - 1], rsem.at[g, half, d - 1], along(half, phase, d))

    def phase_wait(buf, g, phase, steps):
        ssem, rsem = (p1s, p1r) if phase == 1 else (p2s, p2r)
        for half in range(2):
            for d in steps:
                arrive(piece(buf, half, phase, -d, *span(g, half)), ssem.at[g, half, d - 1], rsem.at[g, half, d - 1])

    def relay_start(buf, g):
        for half in range(2):
            r, n = span(g, half)
            for side, d in ((0, 1), (1, 3)):
                arrive(piece(buf, half, 2, -d, r, n), p2s.at[g, half, d - 1], p2r.at[g, half, d - 1])
                part = piece(buf, half, 2, -d, r + side * (n // 2), n // 2)
                send(part, part, rls.at[g, half, side], rlr.at[g, half, side], along(half, 2, d))

    def relay_wait(buf, g):
        for half in range(2):
            r, n = span(g, half)
            for side in range(2):
                arrive(piece(buf, half, 2, 2, r + side * (n // 2), n // 2), rls.at[g, half, side], rlr.at[g, half, side])

    low, high = pl.ds(0, 128), pl.ds(128, 128)
    moves = [(bp_in, bp_ref), (bs_in, bs), (gain_in, gain)]
    moves += [(shard, wc.at[x, y, k, m]) for m, shard in enumerate((cq, ck, cv))]
    for r, shard in ((0, co), (512, lo)):
        moves += [(shard.at[half, :], wp.at[x, y, pl.ds(r, 128), half]) for half in (low, high)]
    moves += [(shard, wp.at[x, y, pl.ds(128 * (m + 1), 128), :]) for m, shard in enumerate((lq, lk, lv))]
    loads = [pltpu.make_async_copy(src, dst, bs_sem.at[n]) for n, (src, dst) in enumerate(moves)]
    for copy in loads:
        copy.start()

    barrier = pltpu.get_barrier_semaphore()
    beside = [wrap(c + 1, SIDE * SIDE), wrap(c - 1, SIDE * SIDE)]
    peers = [dev(wrap(x + d, SIDE), y, k, z) for d in (1, 2, 3)]
    peers += [dev(x, wrap(y + d, SIDE), k, z) for d in (1, 2, 3)]
    peers += [partner, up, down, above, below]
    peers += [(chip * 2 + core, z) for chip in beside for core in (0, 1)]
    for peer in peers:
        pl.semaphore_signal(barrier, inc=1, device_id=peer, device_id_type=MESH)
    loads[0].wait()
    slot_row = bp_ref[...] - (seq * 128 - 64)

    def slots(first, count):
        shape = (ROWS, count)
        return lax.broadcasted_iota(jnp.int32, shape, 0) == slot_row[:, first : first + count]

    ones = slots(0, bs.shape[0]).astype(F32)
    count = jnp.maximum(jnp.sum(ones, axis=1, keepdims=True), 1.0)
    onehot[...] = ones.astype(BF)
    loads[1].wait()

    @pl.loop(0, 4)
    def _(i):
        cols = pl.ds(pl.multiple_of(i * 256, 256), 256)
        pooled[:, cols] = (dot(onehot[...], bs[:, cols]) / count).astype(BF)

    for copy in loads[2:]:
        copy.wait()
    pl.semaphore_wait(barrier, len(peers))

    def wc_piece(half, q, d):
        px, py = (wrap(x - q, SIDE), wrap(y - d, SIDE)) if half == 0 else (wrap(x - d, SIDE), wrap(y - q, SIDE))
        return wc.at[px, py, k, :, pl.ds(*span(0, half)), :]

    def wc_on(q):
        for half in range(2):
            held = wc_piece(half, q, 0)
            for d in (2, 1, 3):
                send(held, held, wcs.at[half, d - 1, q], wcr.at[half, d - 1, q], along(half, 2, d))

    phase_start(wc, 0, 1, (1, 3, 2))
    wc_on(0)
    phase_start(wp, 1, 1, (1, 3, 2))

    def hand_over(half, d):
        held = piece(wc, half, 2, -d, *span(0, half))
        send(held, held, es.at[7 + 4 * half + d], er.at[7 + 4 * half + d], partner)

    for d in (1, 3, 2):
        phase_wait(wc, 0, 1, (d,))
        wc_on(d)
    for half in range(2):
        hand_over(half, 0)
    phase_wait(wp, 1, 1, (1, 2, 3))
    phase_start(wp, 1, 2, (1, 3))
    for d in (1, 3, 2):
        for half in range(2):
            for q in range(SIDE):
                arrive(wc_piece(half, q, d), wcs.at[half, d - 1, q], wcr.at[half, d - 1, q])
            hand_over(half, d)
    relay_start(wp, 1)
    for half in range(2):
        for d in range(SIDE):
            rows = pl.ds(*span(0, half))
            if half == 0:
                theirs = wc.at[:, wrap(y - d, SIDE), 1 - k, :, rows, :]
            else:
                theirs = wc.at[wrap(x - d, SIDE), :, 1 - k, :, rows, :]
            arrive(theirs, es.at[7 + 4 * half + d], er.at[7 + 4 * half + d])

    def cross(m):
        return wc[:, :, :, m].reshape(bs.shape[1], 256)

    phase_start(wp, 2, 1, (1, 3, 2))
    query = dot(pooled[...], cross(0)).astype(BF)
    heads, totals = [0.0, 0.0], [0.0, 0.0]
    for i in range(4):
        part = slice(i * 256, (i + 1) * 256)
        key = dot(bs[part, :], cross(1)).astype(BF)
        value = dot(bs[part, :], cross(2)).astype(BF)
        mask = slots(i * 256, 256)
        for h in range(2):
            cols = slice(h * 128, (h + 1) * 128)
            weight = jnp.where(mask, capped(dot_t(query[:, cols], key[:, cols])), 0.0)
            totals[h] = totals[h] + weight[:, 0:128] + weight[:, 128:256]
            heads[h] = heads[h] + dot(weight.astype(BF), value[:, cols])
    for h in range(2):
        total = jnp.sum(totals[h], axis=1, keepdims=True)
        total = jnp.where(total > 0.0, total, 1.0)
        wbuf[k, :, h * 128 : (h + 1) * 128] = (heads[h] / total).astype(BF)

    send(wbuf.at[k], wbuf.at[k], es.at[1], er.at[1], partner)
    near = wrap(c + 2 * k - 1, SIDE * SIDE)
    edge = wbuf.at[k, pl.ds(pl.multiple_of(k * 192, 64), 64), :]
    for core in (0, 1):
        send(edge, e1b.at[1 - k], es.at[2 + core], er.at[3 - k], (near * 2 + core, z))
    arrive(wbuf.at[1 - k], es.at[1], er.at[1])
    xbuf[64:192, :] = wbuf[0, 128:256, :] + wbuf[1, 0:128, :]
    relay_wait(wp, 1)

    def first_late():
        arrive(e1b.at[0], es.at[2], er.at[2])
        arrive(e1b.at[1], es.at[3], er.at[3])
        xbuf[0:64, :] = wbuf[0, 64:128, :] + e1b[0]
        xbuf[192:256, :] = wbuf[1, 128:192, :] + e1b[1]
        phase_wait(wp, 2, 1, (1, 2, 3))
        phase_start(wp, 2, 2, (1, 3))

    def chunk_of(g, j):
        r, n = GROUPS[g]
        return wp[lax.div(j, SIDE), lax.rem(j, SIDE), r : r + n, :]

    def main_slot(side, m):
        return m if side == 0 else 2 * HOPS + m - 1

    def side_slot(side, m):
        return HOPS + m if side == 0 else 3 * HOPS - 1 + m

    def received(w, slot, p):
        rows = slice(p * STRIP, (p + 1) * STRIP)
        arrive(rrecv.at[w, slot, rows], rss.at[w, slot, p], rsr.at[w, slot, p])
        return rrecv[w, slot, rows].astype(F32)

    def give(w, slot, p, value, target):
        rows = slice(p * STRIP, (p + 1) * STRIP)
        rsend[w, slot, rows] = value.astype(BF)
        send(rsend.at[w, slot, rows], rrecv.at[w, slot, rows], rss.at[w, slot, p], rsr.at[w, slot, p], target)

    def reduce_depth(w, part, late, hook, result):
        def share(side, away, rows=slice(0, ROWS)):
            return part(wrap(z + away if side == 0 else z - away, DEPTH), rows)

        def strips(term):
            return [term[p * STRIP : (p + 1) * STRIP] for p in range(PARTS)]

        far, near = (above, below), (up, down)

        def give_step(m, p, mains, sides):
            for side, main in mains.items():
                give(w, main_slot(side, m), p, main, far[side])
            for side in range(2):
                give(w, side_slot(side, m), p, sides[side], near[side])

        for p in ORDER:
            if p == ORDER[2]:
                late()
            rows = slice(p * STRIP, (p + 1) * STRIP)
            give_step(0, p, {0: share(0, 2 * HOPS, rows)}, [share(side, 2 * HOPS - 1, rows) for side in range(2)])
        for m in range(HOPS):
            last = m + 1 == HOPS
            away = 2 * (HOPS - 1 - m)
            terms = [strips(share(side, away)) for side in range(1 if last else 2)]
            sides = None if last else [strips(share(side, away - 1)) for side in range(2)]
            for p in ORDER:
                sums = [received(w, side_slot(side, m), p) for side in range(2)]
                for side in range(2 if m else 1):
                    sums[side] = sums[side] + received(w, main_slot(side, m), p)
                if last:
                    result(slice(p * STRIP, (p + 1) * STRIP), terms[0][p] + sums[0] + sums[1])
                else:
                    give_step(m + 1, p, {side: terms[side][p] + sums[side] for side in range(2)}, [sides[0][p], sides[1][p]])
            hook(m)

    def first_part(j, rows):
        w = chunk_of(1, j)
        return dot(xbuf[rows, 0:128], w[:, 0:128]) + dot(xbuf[rows, 128:256], w[:, 128:256])

    def first_hook(u):
        if u == 1:
            relay_start(wp, 2)
        if u == 2:
            phase_start(wp, 3, 1, (1, 2, 3))

    def pass_on(m, p):
        part = pl.ds(p * STRIP, STRIP)
        for side, far, near in ((0, above, up), (1, below, down)):
            strip = ag.at[wrap(z - 2 * m if side == 0 else z + 2 * m, DEPTH), part]
            if side == 0 or m + 1 < HOPS:
                slot = main_slot(side, m + side)
                send(strip, strip, ags.at[slot, p], agr.at[slot, p], far)
            slot = side_slot(side, m)
            send(strip, strip, ags.at[slot, p], agr.at[slot, p], near)

    def first_result(rows, value):
        ag[z, rows] = value.astype(BF)
        latent[rows] = ag[z, rows]
        pass_on(0, rows.start // STRIP)

    reduce_depth(0, first_part, first_late, first_hook, first_result)

    def project(js, fresh):
        pieces, weights = [], []
        squares = None
        for j in js:
            held = ag[j].astype(F32)
            squares = held * held if squares is None else squares + held * held
            pieces.append((held * gain[pl.ds(2 * j + k, 1), :]).astype(BF))
            weights.append(chunk_of(2, j))
        left = pieces[0] if len(js) == 1 else jnp.concatenate(pieces, axis=1)
        sq[...] = squares if fresh else sq[...] + squares
        for m in range(3):
            rows = [w[m * 128 : (m + 1) * 128, :] for w in weights]
            right = rows[0] if len(js) == 1 else jnp.concatenate(rows, axis=0)
            term = dot(left, right)
            for h in range(2):
                at = (h, slice(None), PLACE[m])
                piece_of = term[:, h * 128 : (h + 1) * 128]
                acc[at] = piece_of if fresh else acc[at] + piece_of

    relay_wait(wp, 2)
    project([z], True)
    def take(j, slot, p):
        arrive(ag.at[j, pl.ds(p * STRIP, STRIP)], ags.at[slot, p], agr.at[slot, p])

    held = None
    for m in range(HOPS):
        mains = [(main_slot(0, m), wrap(z - 2 * (m + 1), DEPTH))]
        if m + 1 < HOPS:
            mains.append((main_slot(1, m + 1), wrap(z + 2 * (m + 1), DEPTH)))
        sides = [(side_slot(0, m), wrap(z - 1 - 2 * m, DEPTH)), (side_slot(1, m), wrap(z + 1 + 2 * m, DEPTH))]
        for p in ORDER:
            if m + 1 == HOPS and p == ORDER[-1]:
                for slot, j in sides:
                    for strip in range(PARTS):
                        take(j, slot, strip)
                project([j for _, j in sides], False)
            for slot, j in mains:
                take(j, slot, p)
            if m + 1 < HOPS:
                pass_on(m + 1, p)
            if p == ORDER[0] and held is not None:
                project(held, False)
        if m + 1 < HOPS:
            for slot, j in sides:
                for p in range(PARTS):
                    take(j, slot, p)
            project([j for _, j in sides], False)
        held = [j for _, j in mains]
        if m == 1:
            phase_wait(wp, 3, 1, (1, 2, 3))
            phase_start(wp, 3, 2, (1, 3))
    project(held, False)

    acc[1 - k, :, PLACE[3]] = sq[...]
    first, last = (slice(None), pl.ds(0, 384)), (slice(None), pl.ds(384, 128))
    send(acc.at[(1 - k,) + first], e2.at[first], es.at[4], er.at[4], partner)
    send(acc.at[(1 - k,) + last], e2.at[last], es.at[0], er.at[0], partner)
    arrive(e2.at[first], es.at[4], er.at[4])
    mean = jnp.sum(sq[...] + e2[:, PLACE[3]], axis=1, keepdims=True) / (2 * DEPTH * 128)
    factor = lax.rsqrt(mean + EPS)

    def joined(m):
        return ((acc[k, :, PLACE[m]] + e2[:, PLACE[m]]) * factor).astype(BF)

    kvb[x, y, :, 0:128] = joined(1)
    kvb[x, y, :, 128:256] = joined(2)

    def kv_piece(half, q, d, r, n):
        px, py = (wrap(x - q, SIDE), wrap(y - d, SIDE)) if half == 0 else (wrap(x - d, SIDE), wrap(y - q, SIDE))
        return kvb.at[px, py, pl.ds(r, n), :]

    def kv_on(q):
        for half in range(2):
            held = kv_piece(half, q, 0, *span(4, half))
            for side, d in ((0, 1), (1, 3)):
                send(held, held, kvs.at[half, side, q], kvr.at[half, side, q], along(half, 2, d))

    def kv_relay(q):
        for half in range(2):
            r, n = span(4, half)
            for side, d in ((0, 1), (1, 3)):
                arrive(kv_piece(half, q, d, r, n), kvs.at[half, side, q], kvr.at[half, side, q])
                part = kv_piece(half, q, d, r + side * (n // 2), n // 2)
                send(part, part, kvs.at[half, 2 + side, q], kvr.at[half, 2 + side, q], along(half, 2, d))

    def kv_last(q):
        for half in range(2):
            r, n = span(4, half)
            for side in range(2):
                part = kv_piece(half, q, 2, r + side * (n // 2), n // 2)
                arrive(part, kvs.at[half, 2 + side, q], kvr.at[half, 2 + side, q])

    phase_start(kvb, 4, 1, (1, 3, 2))
    kv_on(0)
    arrive(e2.at[last], es.at[0], er.at[0])
    qs[...] = joined(0)

    def attend(blocks):
        value = total = None
        for dx, dy in blocks:
            px, py = wrap(x + dx, SIDE), wrap(y + dy, SIDE)
            weight = capped(dot_t(qs[...], kvb[px, py, :, 0:128]))
            if (dx, dy) == (0, 0):
                shape = (ROWS, ROWS)
                seen = lax.broadcasted_iota(jnp.int32, shape, 1) <= lax.broadcasted_iota(jnp.int32, shape, 0)
                weight = jnp.where(seen, weight, 0.0)
            else:
                weight = weight * jnp.where(px * SIDE + py < c, 1.0, 0.0)
            term = dot(weight.astype(BF), kvb[px, py, :, 128:256])
            mass = weight[:, 0:128] + weight[:, 128:256]
            value = term if value is None else value + term
            total = mass if total is None else total + mass
        own = blocks[0] == (0, 0)
        oacc[...] = value if own else oacc[...] + value
        lacc[...] = total if own else lacc[...] + total

    attend([(0, 0)])
    for d in (1, 3):
        phase_wait(kvb, 4, 1, (d,))
        kv_on(d)
    kv_relay(0)
    phase_wait(kvb, 4, 1, (2,))
    kv_on(2)
    attend([(1, 0), (3, 0), (0, 1), (0, 3)])
    kv_relay(1)
    kv_relay(3)
    attend([(1, 1), (1, 3), (3, 1), (3, 3)])
    kv_relay(2)
    relay_start(wp, 3)
    kv_last(0)
    attend([(2, 0), (0, 2)])
    kv_last(1)
    kv_last(3)
    attend([(2, 1), (2, 3), (1, 2), (3, 2)])
    kv_last(2)
    attend([(2, 2)])
    relay_wait(wp, 3)

    total = jnp.sum(lacc[...], axis=1, keepdims=True)
    att[k] = (oacc[...] / total).astype(BF)
    send(att.at[k], att.at[k], es.at[5], er.at[5], partner)
    arrive(att.at[1 - k], es.at[5], er.at[5])

    def second_part(j, rows):
        w = chunk_of(3, j)
        return dot(att[0, rows], w[:, 0:128]) + dot(att[1, rows], w[:, 128:256])

    def second_result(rows, value):
        fin_s[rows] = (latent[rows].astype(F32) + value).astype(BF)

    reduce_depth(1, second_part, lambda: None, lambda m: None, second_result)
    theirs = fin_s.at[pl.ds(pl.multiple_of((1 - k) * 128, 128), 128), :]
    send(theirs, fin_r, es.at[6], er.at[6], partner)
    mine = pl.ds(pl.multiple_of(k * 128, 128), 128)
    out_ref[:, mine] = fin_s[mine, :]
    arrive(fin_r, es.at[6], er.at[6])
    out_ref[:, pl.ds(pl.multiple_of((1 - k) * 128, 128), 128)] = fin_r[...]
    for copy in started:
        copy.wait_send()


def per_device(
    byte_states, byte_patch, patch_len, cross_query, cross_key, cross_value, cross_out, norm_gain,
    latent_query, latent_key, latent_value, latent_out,
):
    vmem = pl.BlockSpec(memory_space=pltpu.VMEM)
    bytes_here, width = byte_states.shape
    dma = pltpu.SemaphoreType.DMA
    groups = len(GROUPS)
    block = (ROWS, HEAD_DIM)
    return pl.pallas_call(
        kernel,
        out_shape=jax.ShapeDtypeStruct((128, 256), BF),
        in_specs=[pl.BlockSpec(memory_space=pl.ANY)] * 11,
        out_specs=vmem,
        scratch_shapes=[
            pltpu.VMEM((bytes_here, width), BF),
            pltpu.VMEM((1, bytes_here), jnp.int32),
            pltpu.VMEM((2 * DEPTH, HEAD_DIM), F32),
            pltpu.VMEM((SIDE, SIDE, PACKED, 256), BF),
            pltpu.VMEM((SIDE, SIDE, 2, 3, 32, 256), BF),
            pltpu.VMEM((ROWS, width), BF),
            pltpu.VMEM((ROWS, bytes_here), BF),
            pltpu.VMEM((2, ROWS, 256), BF),
            pltpu.VMEM((2, 64, 256), BF),
            pltpu.VMEM((ROWS, 256), BF),
            pltpu.VMEM((2, DEPTH - 1) + block, BF),
            pltpu.VMEM((2, DEPTH - 1) + block, BF),
            pltpu.VMEM((DEPTH,) + block, BF),
            pltpu.VMEM((2, ROWS, 512), F32),
            pltpu.VMEM(block, F32),
            pltpu.VMEM((ROWS, 512), F32),
            pltpu.VMEM(block, BF),
            pltpu.VMEM((SIDE, SIDE, ROWS, 256), BF),
            pltpu.VMEM(block, F32),
            pltpu.VMEM(block, F32),
            pltpu.VMEM((2,) + block, BF),
            pltpu.VMEM(block, BF),
            pltpu.VMEM(block, BF),
            pltpu.VMEM((128, HEAD_DIM), BF),
            dma((13,)),
            dma((groups, 2, 3)),
            dma((groups, 2, 3)),
            dma((groups, 2, 3)),
            dma((groups, 2, 3)),
            dma((groups, 2, 2)),
            dma((groups, 2, 2)),
            dma((2, DEPTH - 1, PARTS)),
            dma((2, DEPTH - 1, PARTS)),
            dma((DEPTH - 1, PARTS)),
            dma((DEPTH - 1, PARTS)),
            dma((15,)),
            dma((15,)),
            dma((2, SIDE, SIDE)),
            dma((2, SIDE, SIDE)),
            dma((2, SIDE - 1, SIDE)),
            dma((2, SIDE - 1, SIDE)),
        ],
        compiler_params=pltpu.CompilerParams(
            collective_id=0, has_side_effects=True, vmem_limit_bytes=60 * 1024 * 1024
        ),
        name="patches",
    )(
        byte_states, byte_patch.reshape(1, -1), cross_query, cross_key, cross_value, cross_out,
        norm_gain.reshape(-1, HEAD_DIM), latent_query, latent_key, latent_value, latent_out,
    )


def solution(mesh):
    return jax.shard_map(
        per_device,
        mesh=mesh,
        in_specs=(
            P("seq", None), P("seq"), P(), P("seq", "tensor"), P("seq", "tensor"), P("seq", "tensor"),
            P("tensor", "seq"), P(), P("seq", "tensor"), P("seq", "tensor"), P("seq", "tensor"), P("tensor", "seq"),
        ),
        out_specs=P("seq", "tensor"),
        check_vma=False,
    )
```
